32 devices in a mesh: groups: 2 (over y), seq: 4 (over z), head: 2 (over x), sub: 2 (over core).
Axes of the slice: x: 2, y: 2, z: 4, core: 2. Of those that a mesh axis runs over, the one named last changes fastest.
Arguments:
- frames_in: bfloat16 [2048, 1536], P(('groups', 'seq', 'head', 'sub')), parts along dimension 0, may hold values from -30 to 30
- attn_gain: float32 [1536], replicated, may hold values from 0.25 to 1.75
- w_qkv: bfloat16 [1536, 24, 192], P(None, ('head', 'sub')), may hold values from -1 to 1
- w_out: bfloat16 [1536, 1536], P(('head', 'sub')), may hold values from -0.3125 to 0.3125
- vit_gain: float32 [1536], replicated, may hold values from 0.25 to 1.75
- w_pair: bfloat16 [2, 1536, 1024], P(None, None, ('head', 'sub')), may hold values from -0.109375 to 0.109375
- w_act: float32 [1024, 7], P(('head', 'sub')), may hold values from -0.375 to 0.375
- pair_frames: int32 [4, 15], P('groups'), parts along dimension 0, may hold values from 0 to 14, each once within a row
Outputs:
- hidden: bfloat16 [2048, 1536], P(('groups', 'seq', 'head', 'sub')), parts along dimension 0
- actions: float32 [4, 15, 7], P('groups'), parts along dimension 0
The draws below stay inside these ranges and needn't reach their ends.
There are 2 independent parts, one for each index of `groups`. The reference program is written for one: setup_inputs(seed, part) draws one part's arguments, and reference() takes and returns one part's arrays. A program takes and returns all parts, laid end to end along the dimension named above; an argument that names none is the same for every part. Nothing has to cross between parts.
All inputs are finite; a program needn't handle non-finite values.
Results may differ from the reference program's by a relative error of at most 0.01.
Values may be sent and summed in bfloat16 or wider, within the bound.
No kernel may reach another device: no remote copies, remote signals or barrier semaphores. Data moves between devices by JAX's collectives and lax.ppermute only.
A program may use at most 64 MiB of HBM per device.

```python
import math
import jax
import jax.numpy as jnp
from jax import lax

HEADS = 24
HEAD_DIM = 64
D = 1536
E = 1024
A = 7
F = 16
ROLLS = 2
P_SIZE = 32
TOKENS = 1024
N_HEAD = 2
N_SUB = 2


def draw_frames_in(key, part):
    key_noise = jax.random.fold_in(key, 11)
    key_row = jax.random.fold_in(key, 12)
    key_col = jax.random.fold_in(key, 13)
    columns = TOKENS // F
    noise_part = jax.random.normal(key_noise, (F, columns, D), jnp.float32)
    row_scale = jnp.exp(jax.random.uniform(key_row, (F, columns, 1), jnp.float32, math.log(0.3), math.log(3.0)))
    col_scale = jnp.exp(jax.random.uniform(key_col, (1, 1, D), jnp.float32, math.log(0.3), math.log(3.0)))
    base_part = noise_part
    values_out = jnp.clip(row_scale * col_scale * base_part, -30.0, 30.0)
    return values_out.reshape(TOKENS, D).astype(jnp.bfloat16)


def draw_w_qkv(key, part):
    key_base = jax.random.fold_in(key, 21)
    base_part = jax.random.normal(key_base, (D, HEADS, 3 * HEAD_DIM), jnp.float32) * D ** (-0.5)
    return jnp.clip(base_part, -1.0, 1.0).astype(jnp.bfloat16)


def steps_of(own_key, shape, shards, low, high):
    def one(dim, parts):
        heights = jax.random.uniform(jax.random.fold_in(jax.random.fold_in(own_key, 6), dim), (parts,), jnp.float32, low / len(shards), high / len(shards))
        return jnp.repeat(jnp.exp(heights), shape[dim] // parts).reshape((-1,) + (1,) * (len(shape) - dim - 1))

    gain = one(*shards[0])
    for cut in shards[1:]:
        gain = gain * one(*cut)
    return gain


def bell_draw(rng, shape, deviation, most, cuts=(), kind=jnp.bfloat16):
    drawn = jax.random.normal(rng, shape, jnp.float32) * deviation
    if len(cuts) > 0:
        drawn = steps_of(rng, shape, cuts, -0.22, 0.18) * drawn
    return jnp.clip(drawn, min=-most, max=most).astype(kind)


def setup_inputs(seed: int = 0, part: int = 0) -> dict:
    arg_keys = jax.random.split(jax.random.key(seed), 9)
    own_keys = jax.random.split(jax.random.fold_in(arg_keys[8], part), 9)
    frames_in = draw_frames_in(jax.random.fold_in(jax.random.fold_in(arg_keys[8], part), 71), part)
    attn_gain = jnp.clip(1.0 + 0.15 * jax.random.normal(arg_keys[1], (D,), jnp.float32), 0.25, 1.75)
    w_qkv = draw_w_qkv(jax.random.fold_in(arg_keys[8], 71), part)
    w_out = bell_draw(arg_keys[3], (D, D), (D // 4) ** -0.5, 0.3125, ((0, 4),))
    vit_gain = jnp.clip(1.0 + 0.15 * jax.random.normal(arg_keys[4], (D,), jnp.float32), 0.25, 1.75)
    w_pair = bell_draw(arg_keys[5], (2, D, E), (2 * D) ** -0.5, 0.109375, ((2, 4),))
    w_act = bell_draw(arg_keys[6], (E, A), (E // 4) ** -0.5, 0.375, ((0, 4),), jnp.float32)
    pair_frames = jax.vmap(lambda own: jax.random.permutation(own, F - 1))(jax.random.split(own_keys[7], ROLLS)).reshape((ROLLS, F - 1)).astype(jnp.int32)
    return dict(frames_in=frames_in, attn_gain=attn_gain, w_qkv=w_qkv, w_out=w_out, vit_gain=vit_gain, w_pair=w_pair, w_act=w_act, pair_frames=pair_frames)


def normalize(values_in, gain_vec):
    floats = values_in.astype(jnp.float32)
    mean_sq = lax.optimization_barrier(jnp.mean(floats * floats, axis=-1, keepdims=True))
    return (floats * lax.rsqrt(mean_sq + 1e-06) * gain_vec).astype(jnp.bfloat16)

def reference(frames_in, attn_gain, w_qkv, w_out, vit_gain, w_pair, w_act, pair_frames):
    columns = TOKENS // F
    normed = normalize(frames_in, attn_gain)
    qkv_rows = jnp.dot(normed, w_qkv.reshape(D, HEADS * 3 * HEAD_DIM), preferred_element_type=jnp.float32).astype(jnp.bfloat16)
    qkv_rows = qkv_rows.reshape(F, columns, HEADS, 3 * HEAD_DIM)
    queries = qkv_rows[..., :HEAD_DIM].astype(jnp.float32)
    key_part = qkv_rows[..., HEAD_DIM:2 * HEAD_DIM].astype(jnp.float32)
    value_part = qkv_rows[..., 2 * HEAD_DIM:].astype(jnp.float32)
    scores = jnp.einsum('fchd,gchd->chfg', queries, key_part) * HEAD_DIM ** (-0.5)
    row_peak = lax.optimization_barrier(jnp.max(scores, axis=-1, keepdims=True))
    weights = jnp.exp(scores - row_peak)
    weights = (weights / lax.optimization_barrier(jnp.sum(weights, axis=-1, keepdims=True))).astype(jnp.bfloat16)
    mixed_out = jnp.einsum('chfg,gchd->fchd', weights.astype(jnp.float32), value_part).astype(jnp.bfloat16)
    mixed_out = mixed_out.reshape(TOKENS, D)
    group_count = N_HEAD * N_SUB
    group_rows = D // group_count
    branch = jnp.zeros((TOKENS, D), jnp.float32)
    for group in range(group_count):
        product = jnp.dot(mixed_out[:, group * group_rows:(group + 1) * group_rows], w_out[group * group_rows:(group + 1) * group_rows], preferred_element_type=jnp.float32)
        rounded = lax.optimization_barrier(product.astype(jnp.bfloat16))
        branch = branch + rounded.astype(jnp.float32)
    hidden = (frames_in.astype(jnp.float32) + branch).astype(jnp.bfloat16)
    vit_in = normalize(hidden, vit_gain).reshape(F, columns, D)
    current = jnp.dot(vit_in[:-1].reshape(-1, D), w_pair[0], preferred_element_type=jnp.float32)
    following = jnp.dot(vit_in[1:].reshape(-1, D), w_pair[1], preferred_element_type=jnp.float32)
    activated = jax.nn.gelu(current + following, approximate=False)
    pooled = lax.optimization_barrier(jnp.mean(activated.reshape(F - 1, ROLLS, P_SIZE, E), axis=2))
    pooled = jnp.transpose(pooled, (1, 0, 2))
    chosen = jnp.take_along_axis(pooled, pair_frames[:, :, None].astype(jnp.int32), axis=1)
    actions = jnp.einsum('rje,ea->rja', chosen, w_act, precision=lax.Precision.HIGHEST)
    return (hidden, actions)
```

```python
import functools

import jax
import jax.numpy as jnp
from jax import lax
from jax.experimental import pallas as pl
from jax.experimental.pallas import tpu as pltpu
from jax.sharding import PartitionSpec as P

F = 16
ROLLS = 2
EPS = 1e-06


def from_behind(value, axis, steps):
    count = lax.axis_size(axis)
    leading, last = (max(0, -steps), min(count, count - steps))
    return lax.ppermute(value, axis, [(source, source + steps) for source in range(leading, last)])


def normalize(values_in, gain_vec):
    floats = values_in.astype(jnp.float32)
    mean_sq = jnp.mean(floats * floats, axis=-1, keepdims=True)
    return (floats * lax.rsqrt(mean_sq + 1e-06) * gain_vec).astype(jnp.bfloat16)


def general_shards(frames_in, attn_gain, w_qkv, w_out, vit_gain, w_pair, w_act, pair_frames):
    rows_own = frames_in.shape[0]
    model_width = frames_in.shape[1]
    seq_count = lax.axis_size("seq")
    split_count = lax.axis_size(("head", "sub"))
    block_rows = rows_own * split_count
    total_cols = block_rows * seq_count // F
    frames_local = max(1, F // seq_count)
    cols_local = block_rows // frames_local
    frame_step = max(1, seq_count // F)
    heads_local = w_qkv.shape[1]
    triple_dim = w_qkv.shape[2]
    head_dim = triple_dim // 3
    qkv_matrix = w_qkv.reshape(model_width, heads_local * triple_dim)
    normed = lax.all_gather(normalize(frames_in, attn_gain), ("head", "sub"), axis=0, tiled=True)
    qkv_rows = jnp.dot(normed, qkv_matrix, preferred_element_type=jnp.float32).astype(jnp.bfloat16)
    qkv_rows = qkv_rows.reshape(
        frames_local, seq_count, cols_local // seq_count, heads_local, triple_dim
    )
    columns = lax.all_to_all(qkv_rows, "seq", split_axis=1, concat_axis=0, tiled=True)
    item_count = columns.shape[2]
    by_frame = columns.reshape(F, -1, heads_local, triple_dim)
    queries = by_frame[..., :head_dim]
    key_part = by_frame[..., head_dim : 2 * head_dim]
    value_part = by_frame[..., 2 * head_dim :]
    scores = jnp.einsum(
        "fchd,gchd->chfg", queries, key_part, preferred_element_type=jnp.float32
    ) * head_dim ** (-0.5)
    row_peak = jnp.max(scores, axis=-1, keepdims=True)
    weights = jnp.exp(scores - row_peak)
    weights = (weights / jnp.sum(weights, axis=-1, keepdims=True)).astype(jnp.bfloat16)
    mixed_out = jnp.einsum(
        "chfg,gchd->fchd", weights, value_part, preferred_element_type=jnp.float32
    ).astype(jnp.bfloat16)
    mixed_out = mixed_out.reshape(seq_count * frames_local, 1, item_count, heads_local * head_dim)
    attended = lax.all_to_all(mixed_out, "seq", split_axis=0, concat_axis=1, tiled=True)
    attended = attended.reshape(block_rows, heads_local * head_dim)
    branch_sum = lax.psum_scatter(
        jnp.dot(attended, w_out, preferred_element_type=jnp.float32).astype(jnp.bfloat16),
        ("head", "sub"),
        scatter_dimension=0,
        tiled=True,
    ).astype(jnp.float32)
    hidden = (frames_in.astype(jnp.float32) + branch_sum).astype(jnp.bfloat16)
    vit_own = normalize(hidden, vit_gain)
    vit_rows = lax.all_gather(vit_own, ("head", "sub"), axis=0, tiled=True)
    current = jnp.dot(vit_rows, w_pair[0], preferred_element_type=jnp.float32)
    ahead_proj = jnp.dot(vit_rows, w_pair[1], preferred_element_type=jnp.float32)
    ahead_proj = ahead_proj.reshape(frames_local, cols_local, -1)
    arrived = from_behind(ahead_proj[:1].astype(jnp.bfloat16), "seq", -frame_step).astype(
        jnp.float32
    )
    following = jnp.concatenate([ahead_proj[1:], arrived], axis=0).reshape(block_rows, -1)
    embedded = current + following
    activated = jax.nn.gelu(embedded, approximate=False).reshape(frames_local, cols_local, -1)
    seq_index = lax.axis_index("seq")
    first_token = seq_index * block_rows
    frame_first = first_token // total_cols
    col_first = first_token % total_cols
    patches = total_cols // ROLLS
    roll_ids = (col_first + jnp.arange(cols_local, dtype=jnp.int32)) // patches
    member = (roll_ids[None, :] == jnp.arange(ROLLS, dtype=jnp.int32)[:, None]).astype(
        jnp.float32
    ) / patches
    pooled = jnp.einsum("rp,fpe->fre", member, activated, precision=lax.Precision.HIGHEST)
    scored = jnp.einsum("fre,ea->fra", pooled, w_act, precision=lax.Precision.HIGHEST)
    frame_ids = frame_first + jnp.arange(frames_local, dtype=jnp.int32)
    selector = (pair_frames[:, :, None] == frame_ids[None, None, :]).astype(jnp.float32)
    partial_value = jnp.einsum("rjf,fra->rja", selector, scored, precision=lax.Precision.HIGHEST)
    actions = lax.psum(partial_value, ("seq", "head", "sub"))
    return (hidden, actions)


def swap(value, axis, mask):
    count = lax.axis_size(axis)
    return lax.ppermute(value, axis, [(source, source ^ mask) for source in range(count)])


def scaled(rows, gain_row):
    mean_sq = jnp.mean(rows * rows, axis=-1, keepdims=True)
    return (rows * lax.rsqrt(mean_sq + EPS) * gain_row).astype(jnp.bfloat16)


def attend_kernel(cols, heads, head_dim, *refs):
    *token_refs, gain_ref, wq_a, wq_b, wo_a, wo_b, out_ref, normed_ref, mixed_ref = refs
    step = token_refs[0].shape[0]
    for place, ref in enumerate(token_refs):
        normed_ref[place * step : (place + 1) * step, :] = scaled(
            ref[...].astype(jnp.float32), gain_ref[...]
        )
    rows = normed_ref.shape[0]
    left = lax.broadcasted_iota(jnp.int32, (rows, rows), 0) % cols
    right = lax.broadcasted_iota(jnp.int32, (rows, rows), 1) % cols
    same = left == right
    total = None
    for wq_ref, wo_ref in ((wq_a, wo_a), (wq_b, wo_b)):
        qkv = lax.dot_general(
            normed_ref[...], wq_ref[...], (((1,), (1,)), ((), ())),
            preferred_element_type=jnp.float32,
        ).astype(jnp.bfloat16)
        for head in range(heads):
            base = head * 3 * head_dim
            query = qkv[:, base : base + head_dim]
            key = qkv[:, base + head_dim : base + 2 * head_dim]
            val = qkv[:, base + 2 * head_dim : base + 3 * head_dim]
            scores = lax.dot_general(
                query, key, (((1,), (1,)), ((), ())), preferred_element_type=jnp.float32
            ) * head_dim ** (-0.5)
            scores = jnp.where(same, scores, -jnp.inf)
            weights = jnp.exp(scores - jnp.max(scores, axis=-1, keepdims=True))
            weights = weights / jnp.sum(weights, axis=-1, keepdims=True)
            mixed_ref[:, head * head_dim : (head + 1) * head_dim] = jnp.dot(
                weights.astype(jnp.bfloat16), val, preferred_element_type=jnp.float32
            ).astype(jnp.bfloat16)
        product = jnp.dot(mixed_ref[...], wo_ref[...], preferred_element_type=jnp.float32)
        product = product.astype(jnp.bfloat16).astype(jnp.float32)
        total = product if total is None else total + product
    out_ref[...] = total.astype(jnp.bfloat16)


def pair_kernel(cols, frames, seq_count, split_count, patches, others, *refs):
    place_ref, *refs = refs
    token_refs, refs = refs[:split_count], refs[split_count:]
    own_ref, refs = refs[0], refs[1:]
    other_refs, refs = refs[:others], refs[others:]
    gain_ref, wp_a, wp_b, wa_a, wa_b, pairs_ref, keep_ref, pass_ref, part_ref, *refs = refs
    hidden_ref, cur_ref, fol_ref = refs
    step = token_refs[0].shape[0]
    seq_place = place_ref[0]
    split_place = place_ref[1]
    roll = place_ref[2]
    for place, ref in enumerate(token_refs):
        rows = slice(place * step, (place + 1) * step)
        branch = own_ref[rows, :].astype(jnp.float32)
        for index, other in enumerate(other_refs):
            there = place ^ (2 * (index + 1))
            branch = branch + other[there * step : (there + 1) * step, :].astype(jnp.float32)
        hidden_ref[rows, :] = (ref[...].astype(jnp.float32) + branch).astype(jnp.bfloat16)
    keep_ref[...] = hidden_ref[:step, :]
    pass_ref[...] = hidden_ref[step : 2 * step, :]
    vit = scaled(hidden_ref[...].astype(jnp.float32), gain_ref[...])
    scored = None
    for wp_ref, wa_ref in ((wp_a, wa_a), (wp_b, wa_b)):
        current = jnp.dot(vit, wp_ref[0], preferred_element_type=jnp.float32)
        ahead = jnp.dot(vit, wp_ref[1], preferred_element_type=jnp.float32)
        for split in range(split_count):
            for seq in range(seq_count):
                frame = (seq_place ^ seq) * split_count + (split_place ^ split)
                piece = slice((split * seq_count + seq) * cols, (split * seq_count + seq + 1) * cols)
                place = pl.ds(pl.multiple_of(frame * cols, cols), cols)
                cur_ref[place, :] = current[piece, :]
                fol_ref[place, :] = ahead[piece, :]
        embedded = cur_ref[: (frames - 1) * cols, :] + fol_ref[cols:, :]
        activated = 0.5 * embedded * (1.0 + lax.erf(embedded * (0.5**0.5)))
        pooled = jnp.sum(activated.reshape(frames - 1, cols, -1), axis=1) * (1.0 / patches)
        here = lax.dot_general(
            pooled, wa_ref[...], (((1,), (1,)), ((), ())),
            preferred_element_type=jnp.float32, precision=lax.Precision.HIGHEST,
        )
        scored = here if scored is None else scored + here
    wanted = pairs_ref.shape[0]
    for index in range(pairs_ref.shape[1]):
        chosen = pairs_ref[:, index : index + 1] == lax.broadcasted_iota(
            jnp.int32, (wanted, frames - 1), 1
        )
        one_hot = jnp.where(chosen & (roll == index), 1.0, 0.0)
        part_ref[index] = jnp.dot(
            one_hot, scored, preferred_element_type=jnp.float32, precision=lax.Precision.HIGHEST
        )


def fast_shards(frames_in, attn_gain, w_qkv, w_out, vit_gain, w_pair, w_act, pair_frames):
    rows_own, width = frames_in.shape
    seq_count = lax.axis_size("seq")
    head_count = lax.axis_size("head")
    split_count = head_count * 2
    heads, triple = w_qkv.shape[1:]
    head_dim = triple // 3
    wide = rows_own // seq_count
    cols = wide // 2
    patches = rows_own // ROLLS
    seq_place = lax.axis_index("seq")
    split_place = lax.axis_index(("head", "sub"))
    sub_place = lax.axis_index("sub")
    wq_own = jnp.transpose(w_qkv, (1, 2, 0)).reshape(heads * triple, width)
    wq_pal = swap(wq_own, "sub", 1)
    wo_pal = swap(w_out, "sub", 1)
    wp_pal = swap(w_pair, "sub", 1)
    wa_own = w_act.T
    wa_pal = swap(wa_own, "sub", 1)
    by_col = frames_in.reshape(seq_count, wide, width)
    pieces = [
        lax.dynamic_index_in_dim(by_col, seq_place ^ step, 0, keepdims=False)
        for step in range(seq_count)
    ]
    pieces = [pieces[0]] + [swap(pieces[step], "seq", step) for step in range(1, seq_count)]
    halves = jnp.stack(pieces).reshape(seq_count, 2, cols, width)
    mine = lax.dynamic_index_in_dim(halves, sub_place, 1, keepdims=False)
    pals = lax.dynamic_index_in_dim(halves, 1 - sub_place, 1, keepdims=False)
    mine = mine.reshape(seq_count * cols, width)
    pals = pals.reshape(seq_count * cols, width)
    tokens = [mine] + [
        swap(pals if step & 1 else mine, ("head", "sub"), step) for step in range(1, split_count)
    ]
    rows = split_count * seq_count * cols
    branch = pl.pallas_call(
        functools.partial(attend_kernel, cols, heads, head_dim),
        out_shape=jax.ShapeDtypeStruct((rows, width), jnp.bfloat16),
        scratch_shapes=[
            pltpu.VMEM((rows, width), jnp.bfloat16),
            pltpu.VMEM((rows, heads * head_dim), jnp.bfloat16),
        ],
    )(*tokens, attn_gain.reshape(1, -1), wq_own, wq_pal, w_out, wo_pal)
    others = [swap(branch, "head", step) for step in range(1, head_count)]
    embed = w_pair.shape[2]
    roll = (seq_place * wide + sub_place * cols) // patches
    places = jnp.stack([seq_place, split_place, roll]).astype(jnp.int32)
    wanted = pair_frames.shape[1]
    actions_dim = w_act.shape[1]
    kept, passed, part = pl.pallas_call(
        functools.partial(
            pair_kernel, cols, F, seq_count, split_count, patches, head_count - 1
        ),
        in_specs=[pl.BlockSpec(memory_space=pltpu.SMEM)]
        + [pl.BlockSpec(memory_space=pltpu.VMEM)] * (split_count + head_count + 6),
        out_shape=(
            jax.ShapeDtypeStruct((seq_count * cols, width), jnp.bfloat16),
            jax.ShapeDtypeStruct((seq_count * cols, width), jnp.bfloat16),
            jax.ShapeDtypeStruct((ROLLS, wanted, actions_dim), jnp.float32),
        ),
        scratch_shapes=[
            pltpu.VMEM((rows, width), jnp.bfloat16),
            pltpu.VMEM((rows, embed), jnp.float32),
            pltpu.VMEM((rows, embed), jnp.float32),
        ],
    )(
        places, *tokens, branch, *others, vit_gain.reshape(1, -1), w_pair, wp_pal, wa_own, wa_pal,
        pair_frames.T,
    )
    arrived = swap(passed, "sub", 1)
    kept = kept.reshape(seq_count, cols, width)
    arrived = arrived.reshape(seq_count, cols, width)
    first = jnp.where(sub_place == 0, kept, arrived)
    second = jnp.where(sub_place == 0, arrived, kept)
    blocks = jnp.concatenate([first, second], axis=1)
    hidden = jnp.zeros((seq_count, wide, width), jnp.bfloat16)
    for step in range(seq_count):
        block = blocks[step] if step == 0 else swap(blocks[step], "seq", step)
        hidden = lax.dynamic_update_index_in_dim(hidden, block, seq_place ^ step, 0)
    hidden = hidden.reshape(rows_own, width)
    actions = part
    actions = sum(
        (swap(actions, ("head", "sub"), step) for step in range(1, split_count)), actions
    )
    actions = sum((swap(actions, "seq", step) for step in range(1, seq_count)), actions)
    return hidden, actions


def shards(frames_in, attn_gain, w_qkv, w_out, vit_gain, w_pair, w_act, pair_frames):
    seq_count = lax.axis_size("seq")
    head_count = lax.axis_size("head")
    rows_own = frames_in.shape[0]
    powers = all(count & (count - 1) == 0 for count in (seq_count, head_count))
    one_frame = seq_count * head_count * lax.axis_size("sub") == F
    tiled = rows_own % (seq_count * 16) == 0 and lax.axis_size("sub") == 2
    chosen = fast_shards if powers and one_frame and tiled else general_shards
    return chosen(frames_in, attn_gain, w_qkv, w_out, vit_gain, w_pair, w_act, pair_frames)


def solution(mesh):
    in_specs = (
        P(("groups", "seq", "head", "sub"), None),
        P(),
        P(None, ("head", "sub"), None),
        P(("head", "sub"), None),
        P(),
        P(None, None, ("head", "sub")),
        P(("head", "sub"), None),
        P("groups", None),
    )
    out_specs = (P(("groups", "seq", "head", "sub"), None), P("groups", None, None))
    return jax.shard_map(shards, mesh=mesh, in_specs=in_specs, out_specs=out_specs, check_vma=False)
```

```python
import functools

import jax
import jax.numpy as jnp
from jax import lax
from jax.experimental import pallas as pl
from jax.experimental.pallas import tpu as pltpu
from jax.sharding import PartitionSpec as P

F = 16
ROLLS = 2
EPS = 1e-06


def from_behind(value, axis, steps):
    count = lax.axis_size(axis)
    leading, last = (max(0, -steps), min(count, count - steps))
    return lax.ppermute(value, axis, [(source, source + steps) for source in range(leading, last)])


def normalize(values_in, gain_vec):
    floats = values_in.astype(jnp.float32)
    mean_sq = jnp.mean(floats * floats, axis=-1, keepdims=True)
    return (floats * lax.rsqrt(mean_sq + 1e-06) * gain_vec).astype(jnp.bfloat16)


def general_shards(frames_in, attn_gain, w_qkv, w_out, vit_gain, w_pair, w_act, pair_frames):
    rows_own = frames_in.shape[0]
    model_width = frames_in.shape[1]
    seq_count = lax.axis_size("seq")
    split_count = lax.axis_size(("head", "sub"))
    block_rows = rows_own * split_count
    total_cols = block_rows * seq_count // F
    frames_local = max(1, F // seq_count)
    cols_local = block_rows // frames_local
    frame_step = max(1, seq_count // F)
    heads_local = w_qkv.shape[1]
    triple_dim = w_qkv.shape[2]
    head_dim = triple_dim // 3
    qkv_matrix = w_qkv.reshape(model_width, heads_local * triple_dim)
    normed = lax.all_gather(normalize(frames_in, attn_gain), ("head", "sub"), axis=0, tiled=True)
    qkv_rows = jnp.dot(normed, qkv_matrix, preferred_element_type=jnp.float32).astype(jnp.bfloat16)
    qkv_rows = qkv_rows.reshape(
        frames_local, seq_count, cols_local // seq_count, heads_local, triple_dim
    )
    columns = lax.all_to_all(qkv_rows, "seq", split_axis=1, concat_axis=0, tiled=True)
    item_count = columns.shape[2]
    by_frame = columns.reshape(F, -1, heads_local, triple_dim)
    queries = by_frame[..., :head_dim]
    key_part = by_frame[..., head_dim : 2 * head_dim]
    value_part = by_frame[..., 2 * head_dim :]
    scores = jnp.einsum(
        "fchd,gchd->chfg", queries, key_part, preferred_element_type=jnp.float32
    ) * head_dim ** (-0.5)
    row_peak = jnp.max(scores, axis=-1, keepdims=True)
    weights = jnp.exp(scores - row_peak)
    weights = (weights / jnp.sum(weights, axis=-1, keepdims=True)).astype(jnp.bfloat16)
    mixed_out = jnp.einsum(
        "chfg,gchd->fchd", weights, value_part, preferred_element_type=jnp.float32
    ).astype(jnp.bfloat16)
    mixed_out = mixed_out.reshape(seq_count * frames_local, 1, item_count, heads_local * head_dim)
    attended = lax.all_to_all(mixed_out, "seq", split_axis=0, concat_axis=1, tiled=True)
    attended = attended.reshape(block_rows, heads_local * head_dim)
    branch_sum = lax.psum_scatter(
        jnp.dot(attended, w_out, preferred_element_type=jnp.float32).astype(jnp.bfloat16),
        ("head", "sub"),
        scatter_dimension=0,
        tiled=True,
    ).astype(jnp.float32)
    hidden = (frames_in.astype(jnp.float32) + branch_sum).astype(jnp.bfloat16)
    vit_own = normalize(hidden, vit_gain)
    vit_rows = lax.all_gather(vit_own, ("head", "sub"), axis=0, tiled=True)
    current = jnp.dot(vit_rows, w_pair[0], preferred_element_type=jnp.float32)
    ahead_proj = jnp.dot(vit_rows, w_pair[1], preferred_element_type=jnp.float32)
    ahead_proj = ahead_proj.reshape(frames_local, cols_local, -1)
    arrived = from_behind(ahead_proj[:1].astype(jnp.bfloat16), "seq", -frame_step).astype(
        jnp.float32
    )
    following = jnp.concatenate([ahead_proj[1:], arrived], axis=0).reshape(block_rows, -1)
    embedded = current + following
    activated = jax.nn.gelu(embedded, approximate=False).reshape(frames_local, cols_local, -1)
    seq_index = lax.axis_index("seq")
    first_token = seq_index * block_rows
    frame_first = first_token // total_cols
    col_first = first_token % total_cols
    patches = total_cols // ROLLS
    roll_ids = (col_first + jnp.arange(cols_local, dtype=jnp.int32)) // patches
    member = (roll_ids[None, :] == jnp.arange(ROLLS, dtype=jnp.int32)[:, None]).astype(
        jnp.float32
    ) / patches
    pooled = jnp.einsum("rp,fpe->fre", member, activated, precision=lax.Precision.HIGHEST)
    scored = jnp.einsum("fre,ea->fra", pooled, w_act, precision=lax.Precision.HIGHEST)
    frame_ids = frame_first + jnp.arange(frames_local, dtype=jnp.int32)
    selector = (pair_frames[:, :, None] == frame_ids[None, None, :]).astype(jnp.float32)
    partial_value = jnp.einsum("rjf,fra->rja", selector, scored, precision=lax.Precision.HIGHEST)
    actions = lax.psum(partial_value, ("seq", "head", "sub"))
    return (hidden, actions)


def swap(value, axis, mask):
    count = lax.axis_size(axis)
    return lax.ppermute(value, axis, [(source, source ^ mask) for source in range(count)])


def scaled(rows, gain_row):
    mean_sq = jnp.mean(rows * rows, axis=-1, keepdims=True)
    return (rows * lax.rsqrt(mean_sq + EPS) * gain_row).astype(jnp.bfloat16)


def attend_kernel(cols, heads, head_dim, *refs):
    *token_refs, gain_ref, wq_a, wq_b, wo_a, wo_b, out_ref = refs[:-5]
    normed_ref, mixed_ref, wq_ref, wo_ref, sems = refs[-5:]
    triple = 3 * head_dim
    group = 2 if heads % 2 == 0 else 1
    chunk = group * triple
    copies = []
    for source in (wq_a, wq_b):
        for first in range(0, heads * triple, chunk):
            index = len(copies)
            copies.append(
                pltpu.make_async_copy(
                    source.at[pl.ds(first, chunk), :],
                    wq_ref.at[pl.ds(index * chunk, chunk), :],
                    sems.at[index],
                )
            )
    inner = heads * head_dim
    out_copies = [
        pltpu.make_async_copy(
            source, wo_ref.at[pl.ds(index * inner, inner), :], sems.at[len(copies) + index]
        )
        for index, source in enumerate((wo_a, wo_b))
    ]
    for copy in copies + out_copies:
        copy.start()
    step = token_refs[0].shape[0]
    for place, ref in enumerate(token_refs):
        normed_ref[place * step : (place + 1) * step, :] = scaled(
            ref[...].astype(jnp.float32), gain_ref[...]
        )
    rows = normed_ref.shape[0]
    left = lax.broadcasted_iota(jnp.int32, (rows, rows), 0) % cols
    right = lax.broadcasted_iota(jnp.int32, (rows, rows), 1) % cols
    same = left == right
    for index, copy in enumerate(copies):
        copy.wait()
        qkv = lax.dot_general(
            wq_ref[index * chunk : (index + 1) * chunk, :], normed_ref[...],
            (((1,), (1,)), ((), ())), preferred_element_type=jnp.float32,
        ).astype(jnp.bfloat16)
        for part in range(group):
            base = part * triple
            query = qkv[base : base + head_dim, :]
            key = qkv[base + head_dim : base + 2 * head_dim, :]
            val = qkv[base + 2 * head_dim : base + triple, :]
            scores = lax.dot_general(
                key, query, (((0,), (0,)), ((), ())), preferred_element_type=jnp.float32
            ) * head_dim ** (-0.5)
            scores = jnp.where(same, scores, -jnp.inf)
            weights = jnp.exp(scores - jnp.max(scores, axis=0, keepdims=True))
            weights = weights * (1.0 / jnp.sum(weights, axis=0, keepdims=True))
            head = index * group + part
            mixed_ref[head * head_dim : (head + 1) * head_dim, :] = jnp.dot(
                val, weights.astype(jnp.bfloat16), preferred_element_type=jnp.float32
            ).astype(jnp.bfloat16)
    total = None
    for index, copy in enumerate(out_copies):
        copy.wait()
        rows_in = slice(index * inner, (index + 1) * inner)
        product = lax.dot_general(
            mixed_ref[rows_in, :], wo_ref[rows_in, :], (((0,), (0,)), ((), ())),
            preferred_element_type=jnp.float32,
        ).astype(jnp.bfloat16).astype(jnp.float32)
        total = product if total is None else total + product
    out_ref[...] = total.astype(jnp.bfloat16)


def pair_kernel(cols, frames, seq_count, split_count, patches, others, *refs):
    place_ref, *refs = refs
    token_refs, refs = refs[:split_count], refs[split_count:]
    own_ref, refs = refs[0], refs[1:]
    other_refs, refs = refs[:others], refs[others:]
    gain_ref, wp_a, wp_b, wa_a, wa_b, pairs_ref, keep_ref, pass_ref, part_ref, *refs = refs
    hidden_ref, cur_ref, fol_ref = refs
    step = token_refs[0].shape[0]
    seq_place = place_ref[0]
    split_place = place_ref[1]
    roll = place_ref[2]
    for place, ref in enumerate(token_refs):
        rows = slice(place * step, (place + 1) * step)
        branch = own_ref[rows, :].astype(jnp.float32)
        for index, other in enumerate(other_refs):
            there = place ^ (2 * (index + 1))
            branch = branch + other[there * step : (there + 1) * step, :].astype(jnp.float32)
        hidden_ref[rows, :] = (ref[...].astype(jnp.float32) + branch).astype(jnp.bfloat16)
    keep_ref[...] = hidden_ref[:step, :]
    pass_ref[...] = hidden_ref[step : 2 * step, :]
    vit = scaled(hidden_ref[...].astype(jnp.float32), gain_ref[...])
    scored = None
    for wp_ref, wa_ref in ((wp_a, wa_a), (wp_b, wa_b)):
        current = jnp.dot(vit, wp_ref[0], preferred_element_type=jnp.float32)
        ahead = jnp.dot(vit, wp_ref[1], preferred_element_type=jnp.float32)
        for split in range(split_count):
            for seq in range(seq_count):
                frame = (seq_place ^ seq) * split_count + (split_place ^ split)
                piece = slice((split * seq_count + seq) * cols, (split * seq_count + seq + 1) * cols)
                place = pl.ds(pl.multiple_of(frame * cols, cols), cols)
                cur_ref[place, :] = current[piece, :]
                fol_ref[place, :] = ahead[piece, :]
        embedded = cur_ref[: (frames - 1) * cols, :] + fol_ref[cols:, :]
        activated = 0.5 * embedded * (1.0 + lax.erf(embedded * (0.5**0.5)))
        pooled = jnp.sum(activated.reshape(frames - 1, cols, -1), axis=1) * (1.0 / patches)
        here = lax.dot_general(
            wa_ref[...], pooled, (((1,), (1,)), ((), ())),
            preferred_element_type=jnp.float32, precision=lax.Precision.HIGHEST,
        )
        scored = here if scored is None else scored + here
    asked = pairs_ref.shape[1]
    each = asked // ROLLS
    shape = (frames - 1, asked)
    lane = lax.broadcasted_iota(jnp.int32, shape, 1)
    chosen = pairs_ref[...] == lax.broadcasted_iota(jnp.int32, shape, 0)
    chosen = chosen & (lane >= roll * each) & (lane < (roll + 1) * each)
    part_ref[...] = jnp.zeros_like(part_ref)
    part_ref[: scored.shape[0], :asked] = jnp.dot(
        scored, jnp.where(chosen, 1.0, 0.0),
        preferred_element_type=jnp.float32, precision=lax.Precision.HIGHEST,
    )


def pack_kernel(seq_count, cols, parts, place_ref, kept_ref, arrived_ref, *refs):
    part_refs, block_refs = refs[:parts], refs[parts:]
    lower = place_ref[3] == 0
    width = kept_ref.shape[1]
    total = part_refs[0][...]
    for ref in part_refs[1:]:
        total = total + ref[...]
    high = total.astype(jnp.bfloat16)
    low = (total - high.astype(jnp.float32)).astype(jnp.bfloat16)
    height = total.shape[0]
    for step, block_ref in enumerate(block_refs):
        rows = slice(step * cols, (step + 1) * cols)
        kept = kept_ref[rows, :].astype(jnp.float32)
        arrived = arrived_ref[rows, :].astype(jnp.float32)
        block_ref[:cols, :width] = jnp.where(lower, kept, arrived).astype(jnp.bfloat16)
        block_ref[cols:, :width] = jnp.where(lower, arrived, kept).astype(jnp.bfloat16)
        block_ref[:height, width:] = high
        block_ref[height : 2 * height, width:] = low


def place_kernel(seq_count, wide, place_ref, *refs):
    block_refs, (hidden_ref, actions_ref) = refs[:seq_count], refs[seq_count:]
    width = hidden_ref.shape[1]
    total = None
    for step, ref in enumerate(block_refs):
        first = pl.multiple_of((place_ref[0] ^ step) * wide, wide)
        hidden_ref[pl.ds(first, wide), :] = ref[:, :width]
        height = 8
        part = ref[:height, width:].astype(jnp.float32)
        part = part + ref[height : 2 * height, width:].astype(jnp.float32)
        total = part if total is None else total + part
    turned = total.T
    each, outs = actions_ref.shape[1:]
    for roll in range(ROLLS):
        actions_ref[roll] = turned[roll * each : (roll + 1) * each, :outs]


def fast_shards(frames_in, attn_gain, w_qkv, w_out, vit_gain, w_pair, w_act, pair_frames):
    rows_own, width = frames_in.shape
    seq_count = lax.axis_size("seq")
    head_count = lax.axis_size("head")
    split_count = head_count * 2
    heads, triple = w_qkv.shape[1:]
    head_dim = triple // 3
    wide = rows_own // seq_count
    cols = wide // 2
    patches = rows_own // ROLLS
    seq_place = lax.axis_index("seq")
    split_place = lax.axis_index(("head", "sub"))
    sub_place = lax.axis_index("sub")
    wq_own = jnp.transpose(w_qkv, (1, 2, 0)).reshape(heads * triple, width)
    wq_pal = swap(wq_own, "sub", 1)
    wo_pal = swap(w_out, "sub", 1)
    wp_pal = swap(w_pair, "sub", 1)
    wa_own = w_act.T
    wa_pal = swap(wa_own, "sub", 1)
    by_col = frames_in.reshape(seq_count, wide, width)
    pieces = [
        lax.dynamic_index_in_dim(by_col, seq_place ^ step, 0, keepdims=False)
        for step in range(seq_count)
    ]
    pieces = [pieces[0]] + [swap(pieces[step], "seq", step) for step in range(1, seq_count)]
    halves = jnp.stack(pieces).reshape(seq_count, 2, cols, width)
    mine = lax.dynamic_index_in_dim(halves, sub_place, 1, keepdims=False)
    pals = lax.dynamic_index_in_dim(halves, 1 - sub_place, 1, keepdims=False)
    mine = mine.reshape(seq_count * cols, width)
    pals = pals.reshape(seq_count * cols, width)
    tokens = [mine] + [
        swap(pals if step & 1 else mine, ("head", "sub"), step) for step in range(1, split_count)
    ]
    rows = split_count * seq_count * cols
    vmem = pl.BlockSpec(memory_space=pltpu.VMEM)
    smem = pl.BlockSpec(memory_space=pltpu.SMEM)
    hbm = pl.BlockSpec(memory_space=pl.ANY)
    inner = heads * head_dim
    branch = pl.pallas_call(
        functools.partial(attend_kernel, cols, heads, head_dim),
        in_specs=[vmem] * (split_count + 1) + [hbm] * 4,
        out_shape=jax.ShapeDtypeStruct((rows, width), jnp.bfloat16),
        scratch_shapes=[
            pltpu.VMEM((rows, width), jnp.bfloat16),
            pltpu.VMEM((2 * inner, rows), jnp.bfloat16),
            pltpu.VMEM((6 * inner, width), jnp.bfloat16),
            pltpu.VMEM((2 * inner, width), jnp.bfloat16),
            pltpu.SemaphoreType.DMA((2 * heads + 2,)),
        ],
    )(*tokens, attn_gain.reshape(1, -1), wq_own, wq_pal, w_out, wo_pal)
    others = [swap(branch, "head", step) for step in range(1, head_count)]
    embed = w_pair.shape[2]
    roll = (seq_place * wide + sub_place * cols) // patches
    places = jnp.stack([seq_place, split_place, roll, sub_place]).astype(jnp.int32)
    wanted = pair_frames.shape[1]
    actions_dim = w_act.shape[1]
    block = jax.ShapeDtypeStruct((seq_count * cols, width), jnp.bfloat16)
    kept, passed, part = pl.pallas_call(
        functools.partial(
            pair_kernel, cols, F, seq_count, split_count, patches, head_count - 1
        ),
        in_specs=[smem] + [vmem] * (split_count + head_count + 6),
        out_shape=(block, block, jax.ShapeDtypeStruct((8, 128), jnp.float32)),
        scratch_shapes=[
            pltpu.VMEM((rows, width), jnp.bfloat16),
            pltpu.VMEM((rows, embed), jnp.float32),
            pltpu.VMEM((rows, embed), jnp.float32),
        ],
    )(
        places, *tokens, branch, *others, vit_gain.reshape(1, -1), w_pair, wp_pal, wa_own, wa_pal,
        pair_frames.reshape(1, -1),
    )
    arrived = swap(passed, "sub", 1)
    parts = [part] + [swap(part, ("head", "sub"), step) for step in range(1, split_count)]
    blocks = pl.pallas_call(
        functools.partial(pack_kernel, seq_count, cols, split_count),
        in_specs=[smem] + [vmem] * (2 + split_count),
        out_shape=[jax.ShapeDtypeStruct((wide, width + 128), jnp.bfloat16)] * seq_count,
    )(places, kept, arrived, *parts)
    blocks = [blocks[0]] + [swap(blocks[step], "seq", step) for step in range(1, seq_count)]
    return pl.pallas_call(
        functools.partial(place_kernel, seq_count, wide),
        in_specs=[smem] + [vmem] * seq_count,
        out_shape=(
            jax.ShapeDtypeStruct((rows_own, width), jnp.bfloat16),
            jax.ShapeDtypeStruct((ROLLS, wanted, actions_dim), jnp.float32),
        ),
    )(places, *blocks)


def shards(frames_in, attn_gain, w_qkv, w_out, vit_gain, w_pair, w_act, pair_frames):
    seq_count = lax.axis_size("seq")
    head_count = lax.axis_size("head")
    rows_own = frames_in.shape[0]
    powers = all(count & (count - 1) == 0 for count in (seq_count, head_count))
    one_frame = seq_count * head_count * lax.axis_size("sub") == F
    tiled = rows_own % (seq_count * 16) == 0 and lax.axis_size("sub") == 2
    tiled = tiled and pair_frames.size <= 128 and w_act.shape[1] <= 8
    chosen = fast_shards if powers and one_frame and tiled else general_shards
    return chosen(frames_in, attn_gain, w_qkv, w_out, vit_gain, w_pair, w_act, pair_frames)


def solution(mesh):
    in_specs = (
        P(("groups", "seq", "head", "sub"), None),
        P(),
        P(None, ("head", "sub"), None),
        P(("head", "sub"), None),
        P(),
        P(None, None, ("head", "sub")),
        P(("head", "sub"), None),
        P("groups", None),
    )
    out_specs = (P(("groups", "seq", "head", "sub"), None), P("groups", None, None))
    return jax.shard_map(shards, mesh=mesh, in_specs=in_specs, out_specs=out_specs, check_vma=False)
```

```python
import functools

import jax
import jax.numpy as jnp
from jax import lax
from jax.experimental import pallas as pl
from jax.experimental.pallas import tpu as pltpu
from jax.sharding import PartitionSpec as P


F = 16
ROLLS = 2
EPS = 1e-06
LINES = 8


def from_behind(value, axis, steps):
    count = lax.axis_size(axis)
    leading, last = (max(0, -steps), min(count, count - steps))
    return lax.ppermute(value, axis, [(source, source + steps) for source in range(leading, last)])


def normalize(values_in, gain_vec):
    floats = values_in.astype(jnp.float32)
    mean_sq = jnp.mean(floats * floats, axis=-1, keepdims=True)
    return (floats * lax.rsqrt(mean_sq + 1e-06) * gain_vec).astype(jnp.bfloat16)


def general_shards(frames_in, attn_gain, w_qkv, w_out, vit_gain, w_pair, w_act, pair_frames):
    rows_own = frames_in.shape[0]
    model_width = frames_in.shape[1]
    seq_count = lax.axis_size("seq")
    split_count = lax.axis_size(("head", "sub"))
    block_rows = rows_own * split_count
    total_cols = block_rows * seq_count // F
    frames_local = max(1, F // seq_count)
    cols_local = block_rows // frames_local
    frame_step = max(1, seq_count // F)
    heads_local = w_qkv.shape[1]
    triple_dim = w_qkv.shape[2]
    head_dim = triple_dim // 3
    qkv_matrix = w_qkv.reshape(model_width, heads_local * triple_dim)
    normed = lax.all_gather(normalize(frames_in, attn_gain), ("head", "sub"), axis=0, tiled=True)
    qkv_rows = jnp.dot(normed, qkv_matrix, preferred_element_type=jnp.float32).astype(jnp.bfloat16)
    qkv_rows = qkv_rows.reshape(
        frames_local, seq_count, cols_local // seq_count, heads_local, triple_dim
    )
    columns = lax.all_to_all(qkv_rows, "seq", split_axis=1, concat_axis=0, tiled=True)
    item_count = columns.shape[2]
    by_frame = columns.reshape(F, -1, heads_local, triple_dim)
    queries = by_frame[..., :head_dim]
    key_part = by_frame[..., head_dim : 2 * head_dim]
    value_part = by_frame[..., 2 * head_dim :]
    scores = jnp.einsum(
        "fchd,gchd->chfg", queries, key_part, preferred_element_type=jnp.float32
    ) * head_dim ** (-0.5)
    row_peak = jnp.max(scores, axis=-1, keepdims=True)
    weights = jnp.exp(scores - row_peak)
    weights = (weights / jnp.sum(weights, axis=-1, keepdims=True)).astype(jnp.bfloat16)
    mixed_out = jnp.einsum(
        "chfg,gchd->fchd", weights, value_part, preferred_element_type=jnp.float32
    ).astype(jnp.bfloat16)
    mixed_out = mixed_out.reshape(seq_count * frames_local, 1, item_count, heads_local * head_dim)
    attended = lax.all_to_all(mixed_out, "seq", split_axis=0, concat_axis=1, tiled=True)
    attended = attended.reshape(block_rows, heads_local * head_dim)
    branch_sum = lax.psum_scatter(
        jnp.dot(attended, w_out, preferred_element_type=jnp.float32).astype(jnp.bfloat16),
        ("head", "sub"),
        scatter_dimension=0,
        tiled=True,
    ).astype(jnp.float32)
    hidden = (frames_in.astype(jnp.float32) + branch_sum).astype(jnp.bfloat16)
    vit_own = normalize(hidden, vit_gain)
    vit_rows = lax.all_gather(vit_own, ("head", "sub"), axis=0, tiled=True)
    current = jnp.dot(vit_rows, w_pair[0], preferred_element_type=jnp.float32)
    ahead_proj = jnp.dot(vit_rows, w_pair[1], preferred_element_type=jnp.float32)
    ahead_proj = ahead_proj.reshape(frames_local, cols_local, -1)
    arrived = from_behind(ahead_proj[:1].astype(jnp.bfloat16), "seq", -frame_step).astype(
        jnp.float32
    )
    following = jnp.concatenate([ahead_proj[1:], arrived], axis=0).reshape(block_rows, -1)
    embedded = current + following
    activated = jax.nn.gelu(embedded, approximate=False).reshape(frames_local, cols_local, -1)
    seq_index = lax.axis_index("seq")
    first_token = seq_index * block_rows
    frame_first = first_token // total_cols
    col_first = first_token % total_cols
    patches = total_cols // ROLLS
    roll_ids = (col_first + jnp.arange(cols_local, dtype=jnp.int32)) // patches
    member = (roll_ids[None, :] == jnp.arange(ROLLS, dtype=jnp.int32)[:, None]).astype(
        jnp.float32
    ) / patches
    pooled = jnp.einsum("rp,fpe->fre", member, activated, precision=lax.Precision.HIGHEST)
    scored = jnp.einsum("fre,ea->fra", pooled, w_act, precision=lax.Precision.HIGHEST)
    frame_ids = frame_first + jnp.arange(frames_local, dtype=jnp.int32)
    selector = (pair_frames[:, :, None] == frame_ids[None, None, :]).astype(jnp.float32)
    partial_value = jnp.einsum("rjf,fra->rja", selector, scored, precision=lax.Precision.HIGHEST)
    actions = lax.psum(partial_value, ("seq", "head", "sub"))
    return (hidden, actions)


GRANT = pltpu.CompilerParams(vmem_limit_bytes=12 * 1024 * 1024)


def on_chip(value):
    return pltpu.with_memory_space_constraint(value, pltpu.VMEM)


def off_chip(value):
    return pltpu.with_memory_space_constraint(value, pltpu.HBM)


def swap(value, axis, mask):
    count = lax.axis_size(axis)
    pairs = [(source, source ^ mask) for source in range(count)]
    return on_chip(lax.ppermute(value, axis, pairs))


def lined(gain_ref):
    return jnp.concatenate([gain_ref[row : row + 1, :] for row in range(gain_ref.shape[0])], axis=1)


def scaled(rows, gain_row):
    mean_sq = jnp.mean(rows * rows, axis=-1, keepdims=True)
    return (rows * lax.rsqrt(mean_sq + EPS) * gain_row).astype(jnp.bfloat16)


def cut_kernel(seq_count, small, tokens_ref, *refs):
    small_refs, out_refs, sems = refs[:small], refs[small:-1], refs[-1]
    wide = out_refs[0].shape[0]
    place = lax.axis_index("seq")
    copies = []
    for step, out_ref in enumerate(out_refs[:seq_count]):
        first = pl.multiple_of((place ^ step) * wide, wide)
        source = tokens_ref.at[pl.ds(first, wide), :]
        copies.append(pltpu.make_async_copy(source, out_ref, sems.at[step]))
    for source, out_ref in zip(small_refs, out_refs[seq_count:]):
        copies.append(pltpu.make_async_copy(source, out_ref, sems.at[len(copies)]))
    for copy in copies:
        copy.start()
    for copy in copies:
        copy.wait()


def halve_kernel(cols, *refs):
    *piece_refs, mine_ref, pals_ref = refs
    for lower, (first_ref, second_ref) in enumerate(((pals_ref, mine_ref), (mine_ref, pals_ref))):

        @pl.when(lax.axis_index("sub") == 1 - lower)
        def _():
            for step, ref in enumerate(piece_refs):
                rows = slice(step * cols, (step + 1) * cols)
                first_ref[rows, :] = ref[:cols, :]
                second_ref[rows, :] = ref[cols:, :]


def attend_kernel(cols, heads, head_dim, *refs):
    *token_refs, gain_ref, wq_far, wq_pal, wo_far, wo_pal, out_ref = refs[:-5]
    normed_ref, mixed_ref, wq_own, wo_own, sems = refs[-5:]
    triple = 3 * head_dim
    inner = heads * head_dim
    group = 2 if heads % 2 == 0 else 1
    chunk = group * triple
    copies = []
    for first in range(0, heads * triple, chunk):
        piece = pl.ds(first, chunk)
        copies.append(
            pltpu.make_async_copy(wq_far.at[piece, :], wq_own.at[piece, :], sems.at[len(copies)])
        )
    copies.append(pltpu.make_async_copy(wo_far, wo_own, sems.at[len(copies)]))
    for copy in copies:
        copy.start()
    step = token_refs[0].shape[0]
    gain_row = lined(gain_ref)
    for place, ref in enumerate(token_refs):
        normed_ref[place * step : (place + 1) * step, :] = scaled(
            ref[...].astype(jnp.float32), gain_row
        )
    rows = normed_ref.shape[0]
    left = lax.broadcasted_iota(jnp.int32, (rows, rows), 0) % cols
    right = lax.broadcasted_iota(jnp.int32, (rows, rows), 1) % cols
    same = left == right
    for index, wq_ref in enumerate((wq_pal, wq_own)):
        for start in range(0, heads, group):
            if index == 1:
                copies[start // group].wait()
            qkv = lax.dot_general(
                wq_ref[start * triple : start * triple + chunk, :], normed_ref[...],
                (((1,), (1,)), ((), ())), preferred_element_type=jnp.float32,
            ).astype(jnp.bfloat16)
            for part in range(group):
                base = part * triple
                query = qkv[base : base + head_dim, :]
                key = qkv[base + head_dim : base + 2 * head_dim, :]
                val = qkv[base + 2 * head_dim : base + triple, :]
                scores = lax.dot_general(
                    key, query, (((0,), (0,)), ((), ())), preferred_element_type=jnp.float32
                ) * head_dim ** (-0.5)
                scores = jnp.where(same, scores, -jnp.inf)
                weights = jnp.exp(scores - jnp.max(scores, axis=0, keepdims=True))
                weights = weights * (1.0 / jnp.sum(weights, axis=0, keepdims=True))
                first = index * inner + (start + part) * head_dim
                mixed_ref[first : first + head_dim, :] = jnp.dot(
                    val, weights.astype(jnp.bfloat16), preferred_element_type=jnp.float32
                ).astype(jnp.bfloat16)
    total = None
    for index, wo_ref in enumerate((wo_pal, wo_own)):
        if index == 1:
            copies[-1].wait()
        product = lax.dot_general(
            mixed_ref[index * inner : (index + 1) * inner, :], wo_ref[...],
            (((0,), (0,)), ((), ())), preferred_element_type=jnp.float32,
        ).astype(jnp.bfloat16).astype(jnp.float32)
        total = product if total is None else total + product
    out_ref[...] = total.astype(jnp.bfloat16)


def pair_kernel(cols, frames, seq_count, split_count, patches, others, *refs):
    token_refs, refs = refs[:split_count], refs[split_count:]
    own_ref, refs = refs[0], refs[1:]
    other_refs, refs = refs[:others], refs[others:]
    gain_ref, wp_a, wp_b, wa_a, wa_b, pairs_ref, keep_ref, pass_ref, part_ref, *refs = refs
    hidden_ref, cur_ref, fol_ref = refs
    step = token_refs[0].shape[0]
    seq_place = lax.axis_index("seq")
    split_place = lax.axis_index(("head", "sub"))
    roll = (seq_place * 2 + lax.axis_index("sub")) * cols // patches
    for place, ref in enumerate(token_refs):
        rows = slice(place * step, (place + 1) * step)
        branch = own_ref[rows, :].astype(jnp.float32)
        for index, other in enumerate(other_refs):
            there = place ^ (2 * (index + 1))
            branch = branch + other[there * step : (there + 1) * step, :].astype(jnp.float32)
        hidden_ref[rows, :] = (ref[...].astype(jnp.float32) + branch).astype(jnp.bfloat16)
    keep_ref[...] = hidden_ref[:step, :]
    pass_ref[...] = hidden_ref[step : 2 * step, :]
    vit = scaled(hidden_ref[...].astype(jnp.float32), lined(gain_ref))
    scored = None
    for wp_ref, wa_ref in ((wp_a, wa_a), (wp_b, wa_b)):
        current = jnp.dot(vit, wp_ref[0], preferred_element_type=jnp.float32)
        ahead = jnp.dot(vit, wp_ref[1], preferred_element_type=jnp.float32)
        for split in range(split_count):
            for seq in range(seq_count):
                frame = (seq_place ^ seq) * split_count + (split_place ^ split)
                piece = slice((split * seq_count + seq) * cols, (split * seq_count + seq + 1) * cols)
                place = pl.ds(pl.multiple_of(frame * cols, cols), cols)
                cur_ref[place, :] = current[piece, :]
                fol_ref[place, :] = ahead[piece, :]
        embedded = cur_ref[: (frames - 1) * cols, :] + fol_ref[cols:, :]
        activated = 0.5 * embedded * (1.0 + lax.erf(embedded * (0.5**0.5)))
        pooled = jnp.sum(activated.reshape(frames - 1, cols, -1), axis=1) * (1.0 / patches)
        here = lax.dot_general(
            wa_ref[...], pooled, (((1,), (1,)), ((), ())),
            preferred_element_type=jnp.float32, precision=lax.Precision.HIGHEST,
        )
        scored = here if scored is None else scored + here
    wanted = pairs_ref.shape[1]
    part_ref[...] = jnp.zeros_like(part_ref)
    for index in range(ROLLS):
        chosen = pairs_ref[index : index + 1, :] == lax.broadcasted_iota(
            jnp.int32, (frames - 1, wanted), 0
        )
        first = index * LINES
        part_ref[first : first + scored.shape[0], :wanted] = jnp.dot(
            scored, jnp.where(chosen & (roll == index), 1.0, 0.0),
            preferred_element_type=jnp.float32, precision=lax.Precision.HIGHEST,
        )


def pack_kernel(cols, parts, kept_ref, arrived_ref, *refs):
    part_refs, block_refs = refs[:parts], refs[parts:]
    width = kept_ref.shape[1]
    total = part_refs[0][...]
    for ref in part_refs[1:]:
        total = total + ref[...]
    high = total.astype(jnp.bfloat16)
    low = (total - high.astype(jnp.float32)).astype(jnp.bfloat16)
    height, lanes = total.shape
    for block_ref in block_refs:
        block_ref[:height, width : width + lanes] = high
        block_ref[:height, width + lanes :] = low
    for lower, (first_ref, second_ref) in enumerate(
        ((arrived_ref, kept_ref), (kept_ref, arrived_ref))
    ):

        @pl.when(lax.axis_index("sub") == 1 - lower)
        def _():
            for step, block_ref in enumerate(block_refs):
                rows = slice(step * cols, (step + 1) * cols)
                block_ref[:cols, :width] = first_ref[rows, :]
                block_ref[cols:, :width] = second_ref[rows, :]


def place_kernel(seq_count, wide, *refs):
    block_refs, (hidden_ref, actions_ref) = refs[:seq_count], refs[seq_count:]
    width = hidden_ref.shape[1]
    lanes = (block_refs[0].shape[1] - width) // 2
    height = ROLLS * LINES
    total = None
    for step, ref in enumerate(block_refs):
        first = pl.multiple_of((lax.axis_index("seq") ^ step) * wide, wide)
        hidden_ref[pl.ds(first, wide), :] = ref[:, :width]
        part = ref[:height, width : width + lanes].astype(jnp.float32)
        part = part + ref[:height, width + lanes :].astype(jnp.float32)
        total = part if total is None else total + part
    outs, _, each = actions_ref.shape
    for roll in range(ROLLS):
        actions_ref[:, roll, :] = total[roll * LINES : roll * LINES + outs, :each]


def fast_shards(frames_in, attn_gain, w_qkv, w_out, vit_gain, w_pair, w_act, pair_frames):
    rows_own, width = frames_in.shape
    seq_count = lax.axis_size("seq")
    head_count = lax.axis_size("head")
    split_count = head_count * 2
    heads, triple = w_qkv.shape[1:]
    head_dim = triple // 3
    wide = rows_own // seq_count
    cols = wide // 2
    patches = rows_own // ROLLS
    vmem = pl.BlockSpec(memory_space=pltpu.VMEM)
    hbm = pl.BlockSpec(memory_space=pltpu.HBM)
    wq_own = jnp.transpose(w_qkv, (1, 2, 0)).reshape(heads * triple, width)
    wa_own = w_act.T
    small = [attn_gain.reshape(-1, 128), vit_gain.reshape(-1, 128), wa_own, pair_frames]
    cut = pl.pallas_call(
        functools.partial(cut_kernel, seq_count, len(small)),
        compiler_params=GRANT,
        in_specs=[hbm] * (1 + len(small)),
        out_specs=[vmem] * (seq_count + len(small)),
        out_shape=[pltpu.VMEM((wide, width), jnp.bfloat16)] * seq_count
        + [pltpu.VMEM(value.shape, value.dtype) for value in small],
        scratch_shapes=[pltpu.SemaphoreType.DMA((seq_count + len(small),))],
    )(off_chip(frames_in), *[off_chip(value) for value in small])
    pieces = cut[:seq_count]
    attn_gain, vit_gain, wa_own, pair_frames = cut[seq_count:]
    pieces = [pieces[0]] + [swap(pieces[step], "seq", step) for step in range(1, seq_count)]
    wq_pal = swap(wq_own, "sub", 1)
    wo_pal = swap(w_out, "sub", 1)
    wp_pal = swap(w_pair, "sub", 1)
    wa_pal = swap(wa_own, "sub", 1)
    half = pltpu.VMEM((seq_count * cols, width), jnp.bfloat16)
    mine, pals = pl.pallas_call(
        functools.partial(halve_kernel, cols),
        compiler_params=GRANT,
        in_specs=[vmem] * seq_count,
        out_specs=[vmem] * 2,
        out_shape=[half] * 2,
    )(*pieces)
    tokens = [mine] + [
        swap(pals if step & 1 else mine, ("head", "sub"), step)
        for step in range(1, split_count)
    ]
    rows = split_count * seq_count * cols
    inner = heads * head_dim
    branch = pl.pallas_call(
        functools.partial(attend_kernel, cols, heads, head_dim),
        compiler_params=GRANT,
        in_specs=[vmem] * (split_count + 1) + [hbm, vmem, hbm, vmem],
        out_specs=vmem,
        out_shape=pltpu.VMEM((rows, width), jnp.bfloat16),
        scratch_shapes=[
            pltpu.VMEM((rows, width), jnp.bfloat16),
            pltpu.VMEM((2 * inner, rows), jnp.bfloat16),
            pltpu.VMEM((3 * inner, width), jnp.bfloat16),
            pltpu.VMEM((inner, width), jnp.bfloat16),
            pltpu.SemaphoreType.DMA((heads + 1,)),
        ],
    )(*tokens, attn_gain, off_chip(wq_own), wq_pal, off_chip(w_out), wo_pal)
    others = [swap(branch, "head", step) for step in range(1, head_count)]
    embed = w_pair.shape[2]
    wanted = pair_frames.shape[1]
    kept, passed, part = pl.pallas_call(
        functools.partial(
            pair_kernel, cols, F, seq_count, split_count, patches, head_count - 1
        ),
        compiler_params=GRANT,
        in_specs=[vmem] * (split_count + head_count + 6),
        out_specs=[vmem] * 3,
        out_shape=(half, half, pltpu.VMEM((ROLLS * LINES, 128), jnp.float32)),
        scratch_shapes=[
            pltpu.VMEM((rows, width), jnp.bfloat16),
            pltpu.VMEM((rows, embed), jnp.float32),
            pltpu.VMEM((rows, embed), jnp.float32),
        ],
    )(
        *tokens, branch, *others, vit_gain, on_chip(w_pair), wp_pal,
        wa_own, wa_pal, pair_frames,
    )
    arrived = swap(passed, "sub", 1)
    parts = [part] + [swap(part, ("head", "sub"), step) for step in range(1, split_count)]
    blocks = pl.pallas_call(
        functools.partial(pack_kernel, cols, split_count),
        compiler_params=GRANT,
        in_specs=[vmem] * (2 + split_count),
        out_specs=[vmem] * seq_count,
        out_shape=[pltpu.VMEM((wide, width + 256), jnp.bfloat16)] * seq_count,
    )(kept, arrived, *parts)
    blocks = [blocks[0]] + [swap(blocks[step], "seq", step) for step in range(1, seq_count)]
    hidden, actions = pl.pallas_call(
        functools.partial(place_kernel, seq_count, wide),
        compiler_params=GRANT,
        in_specs=[vmem] * seq_count,
        out_shape=(
            jax.ShapeDtypeStruct((rows_own, width), jnp.bfloat16),
            jax.ShapeDtypeStruct((w_act.shape[1], ROLLS, wanted), jnp.float32),
        ),
    )(*blocks)
    return hidden, jnp.transpose(actions, (1, 2, 0))


def shards(frames_in, attn_gain, w_qkv, w_out, vit_gain, w_pair, w_act, pair_frames):
    seq_count = lax.axis_size("seq")
    head_count = lax.axis_size("head")
    rows_own = frames_in.shape[0]
    powers = all(count & (count - 1) == 0 for count in (seq_count, head_count))
    one_frame = seq_count * head_count * lax.axis_size("sub") == F
    tiled = rows_own % (seq_count * 16) == 0 and lax.axis_size("sub") == 2
    tiled = tiled and rows_own // seq_count >= ROLLS * LINES
    tiled = tiled and pair_frames.shape[1] <= 128 and w_act.shape[1] <= LINES
    tiled = tiled and frames_in.shape[1] % 128 == 0
    chosen = fast_shards if powers and one_frame and tiled else general_shards
    return chosen(frames_in, attn_gain, w_qkv, w_out, vit_gain, w_pair, w_act, pair_frames)


def solution(mesh):
    in_specs = (
        P(("groups", "seq", "head", "sub"), None),
        P(),
        P(None, ("head", "sub"), None),
        P(("head", "sub"), None),
        P(),
        P(None, None, ("head", "sub")),
        P(("head", "sub"), None),
        P("groups", None),
    )
    out_specs = (P(("groups", "seq", "head", "sub"), None), P("groups", None, None))
    return jax.shard_map(shards, mesh=mesh, in_specs=in_specs, out_specs=out_specs, check_vma=False)
```

```python
import functools

import jax
import jax.numpy as jnp
from jax import lax
from jax.experimental import pallas as pl
from jax.experimental.pallas import tpu as pltpu
from jax.sharding import PartitionSpec as P


F = 16
ROLLS = 2
EPS = 1e-06
LINES = 8


def from_behind(value, axis, steps):
    count = lax.axis_size(axis)
    leading, last = (max(0, -steps), min(count, count - steps))
    return lax.ppermute(value, axis, [(source, source + steps) for source in range(leading, last)])


def normalize(values_in, gain_vec):
    floats = values_in.astype(jnp.float32)
    mean_sq = jnp.mean(floats * floats, axis=-1, keepdims=True)
    return (floats * lax.rsqrt(mean_sq + 1e-06) * gain_vec).astype(jnp.bfloat16)


def general_shards(frames_in, attn_gain, w_qkv, w_out, vit_gain, w_pair, w_act, pair_frames):
    rows_own = frames_in.shape[0]
    model_width = frames_in.shape[1]
    seq_count = lax.axis_size("seq")
    split_count = lax.axis_size(("head", "sub"))
    block_rows = rows_own * split_count
    total_cols = block_rows * seq_count // F
    frames_local = max(1, F // seq_count)
    cols_local = block_rows // frames_local
    frame_step = max(1, seq_count // F)
    heads_local = w_qkv.shape[1]
    triple_dim = w_qkv.shape[2]
    head_dim = triple_dim // 3
    qkv_matrix = w_qkv.reshape(model_width, heads_local * triple_dim)
    normed = lax.all_gather(normalize(frames_in, attn_gain), ("head", "sub"), axis=0, tiled=True)
    qkv_rows = jnp.dot(normed, qkv_matrix, preferred_element_type=jnp.float32).astype(jnp.bfloat16)
    qkv_rows = qkv_rows.reshape(
        frames_local, seq_count, cols_local // seq_count, heads_local, triple_dim
    )
    columns = lax.all_to_all(qkv_rows, "seq", split_axis=1, concat_axis=0, tiled=True)
    item_count = columns.shape[2]
    by_frame = columns.reshape(F, -1, heads_local, triple_dim)
    queries = by_frame[..., :head_dim]
    key_part = by_frame[..., head_dim : 2 * head_dim]
    value_part = by_frame[..., 2 * head_dim :]
    scores = jnp.einsum(
        "fchd,gchd->chfg", queries, key_part, preferred_element_type=jnp.float32
    ) * head_dim ** (-0.5)
    row_peak = jnp.max(scores, axis=-1, keepdims=True)
    weights = jnp.exp(scores - row_peak)
    weights = (weights / jnp.sum(weights, axis=-1, keepdims=True)).astype(jnp.bfloat16)
    mixed_out = jnp.einsum(
        "chfg,gchd->fchd", weights, value_part, preferred_element_type=jnp.float32
    ).astype(jnp.bfloat16)
    mixed_out = mixed_out.reshape(seq_count * frames_local, 1, item_count, heads_local * head_dim)
    attended = lax.all_to_all(mixed_out, "seq", split_axis=0, concat_axis=1, tiled=True)
    attended = attended.reshape(block_rows, heads_local * head_dim)
    branch_sum = lax.psum_scatter(
        jnp.dot(attended, w_out, preferred_element_type=jnp.float32).astype(jnp.bfloat16),
        ("head", "sub"),
        scatter_dimension=0,
        tiled=True,
    ).astype(jnp.float32)
    hidden = (frames_in.astype(jnp.float32) + branch_sum).astype(jnp.bfloat16)
    vit_own = normalize(hidden, vit_gain)
    vit_rows = lax.all_gather(vit_own, ("head", "sub"), axis=0, tiled=True)
    current = jnp.dot(vit_rows, w_pair[0], preferred_element_type=jnp.float32)
    ahead_proj = jnp.dot(vit_rows, w_pair[1], preferred_element_type=jnp.float32)
    ahead_proj = ahead_proj.reshape(frames_local, cols_local, -1)
    arrived = from_behind(ahead_proj[:1].astype(jnp.bfloat16), "seq", -frame_step).astype(
        jnp.float32
    )
    following = jnp.concatenate([ahead_proj[1:], arrived], axis=0).reshape(block_rows, -1)
    embedded = current + following
    activated = jax.nn.gelu(embedded, approximate=False).reshape(frames_local, cols_local, -1)
    seq_index = lax.axis_index("seq")
    first_token = seq_index * block_rows
    frame_first = first_token // total_cols
    col_first = first_token % total_cols
    patches = total_cols // ROLLS
    roll_ids = (col_first + jnp.arange(cols_local, dtype=jnp.int32)) // patches
    member = (roll_ids[None, :] == jnp.arange(ROLLS, dtype=jnp.int32)[:, None]).astype(
        jnp.float32
    ) / patches
    pooled = jnp.einsum("rp,fpe->fre", member, activated, precision=lax.Precision.HIGHEST)
    scored = jnp.einsum("fre,ea->fra", pooled, w_act, precision=lax.Precision.HIGHEST)
    frame_ids = frame_first + jnp.arange(frames_local, dtype=jnp.int32)
    selector = (pair_frames[:, :, None] == frame_ids[None, None, :]).astype(jnp.float32)
    partial_value = jnp.einsum("rjf,fra->rja", selector, scored, precision=lax.Precision.HIGHEST)
    actions = lax.psum(partial_value, ("seq", "head", "sub"))
    return (hidden, actions)


GRANT = pltpu.CompilerParams(vmem_limit_bytes=12 * 1024 * 1024)


def on_chip(value):
    return pltpu.with_memory_space_constraint(value, pltpu.VMEM)


def off_chip(value):
    return pltpu.with_memory_space_constraint(value, pltpu.HBM)


def swap(value, axis, mask):
    count = lax.axis_size(axis)
    pairs = [(source, source ^ mask) for source in range(count)]
    return on_chip(lax.ppermute(value, axis, pairs))


def lined(gain_ref):
    return jnp.concatenate([gain_ref[row : row + 1, :] for row in range(gain_ref.shape[0])], axis=1)


def scaled(rows, gain_row):
    mean_sq = jnp.mean(rows * rows, axis=-1, keepdims=True)
    return (rows * lax.rsqrt(mean_sq + EPS) * gain_row).astype(jnp.bfloat16)


def cut_kernel(seq_count, small, tokens_ref, *refs):
    small_refs, out_refs, sems = refs[:small], refs[small:-1], refs[-1]
    wide = out_refs[0].shape[0]
    place = lax.axis_index("seq")
    copies = []
    for step, out_ref in enumerate(out_refs[:seq_count]):
        first = pl.multiple_of((place ^ step) * wide, wide)
        source = tokens_ref.at[pl.ds(first, wide), :]
        copies.append(pltpu.make_async_copy(source, out_ref, sems.at[step]))
    for source, out_ref in zip(small_refs, out_refs[seq_count:]):
        copies.append(pltpu.make_async_copy(source, out_ref, sems.at[len(copies)]))
    for copy in copies:
        copy.start()
    for copy in copies:
        copy.wait()


def halve_kernel(cols, *refs):
    *piece_refs, mine_ref, pals_ref = refs
    for lower, (first_ref, second_ref) in enumerate(((pals_ref, mine_ref), (mine_ref, pals_ref))):

        @pl.when(lax.axis_index("sub") == 1 - lower)
        def _():
            for step, ref in enumerate(piece_refs):
                rows = slice(step * cols, (step + 1) * cols)
                first_ref[rows, :] = ref[:cols, :]
                second_ref[rows, :] = ref[cols:, :]


def aligned(value, step):
    return value if isinstance(value, int) else pl.multiple_of(value, step)


def each(count, body):
    lax.fori_loop(0, count, lambda index, carry: (body(index), carry)[1], 0)


def attend_kernel(cols, heads, head_dim, *refs):
    *token_refs, gain_ref, wq_far, wq_pal, wo_far, wo_pal, out_ref = refs[:-6]
    normed_ref, qkv_ref, mixed_ref, wq_own, wo_own, sems = refs[-6:]
    triple = 3 * head_dim
    inner = heads * head_dim
    group = 2 if heads % 2 == 0 else 1
    chunk = group * triple

    def fetch(index):
        piece = pl.ds(aligned(index * chunk, chunk), chunk)
        return pltpu.make_async_copy(wq_far.at[piece, :], wq_own.at[piece, :], sems.at[index])

    for index in range(heads // group):
        fetch(index).start()
    fetch_out = pltpu.make_async_copy(wo_far, wo_own, sems.at[heads // group])
    fetch_out.start()
    step = token_refs[0].shape[0]
    gain_row = lined(gain_ref)
    for place, ref in enumerate(token_refs):
        normed_ref[place * step : (place + 1) * step, :] = scaled(
            ref[...].astype(jnp.float32), gain_row
        )
    rows = normed_ref.shape[0]

    def project(wq_ref, source, size, target):
        qkv_ref[pl.ds(aligned(target, head_dim), size), :] = lax.dot_general(
            wq_ref[pl.ds(aligned(source, size), size), :], normed_ref[...],
            (((1,), (1,)), ((), ())), preferred_element_type=jnp.float32,
        ).astype(jnp.bfloat16)

    large = heads * triple // group

    def project_pal(index):
        project(wq_pal, index * large, large, index * large)

    def project_own(index):
        fetch(index).wait()
        project(wq_own, index * chunk, chunk, heads * triple + index * chunk)

    each(group, project_pal)
    each(heads // group, project_own)
    left = lax.broadcasted_iota(jnp.int32, (rows, rows), 0) % cols
    right = lax.broadcasted_iota(jnp.int32, (rows, rows), 1) % cols
    same = left == right
    for head in range(2 * heads):
        base = head * triple
        query = qkv_ref[base : base + head_dim, :]
        key = qkv_ref[base + head_dim : base + 2 * head_dim, :]
        val = qkv_ref[base + 2 * head_dim : base + triple, :]
        scores = lax.dot_general(
            key, query, (((0,), (0,)), ((), ())), preferred_element_type=jnp.float32
        ) * head_dim ** (-0.5)
        scores = jnp.where(same, scores, -jnp.inf)
        weights = jnp.exp(scores - jnp.max(scores, axis=0, keepdims=True))
        weights = weights * (1.0 / jnp.sum(weights, axis=0, keepdims=True))
        mixed_ref[head * head_dim : (head + 1) * head_dim, :] = jnp.dot(
            val, weights.astype(jnp.bfloat16), preferred_element_type=jnp.float32
        ).astype(jnp.bfloat16)
    fetch_out.wait()
    total = None
    for index, wo_ref in enumerate((wo_pal, wo_own)):
        product = lax.dot_general(
            mixed_ref[index * inner : (index + 1) * inner, :], wo_ref[...],
            (((0,), (0,)), ((), ())), preferred_element_type=jnp.float32,
        ).astype(jnp.bfloat16).astype(jnp.float32)
        total = product if total is None else total + product
    out_ref[...] = total.astype(jnp.bfloat16)


def pair_kernel(cols, frames, seq_count, split_count, patches, others, *refs):
    token_refs, refs = refs[:split_count], refs[split_count:]
    own_ref, refs = refs[0], refs[1:]
    other_refs, refs = refs[:others], refs[others:]
    gain_ref, wp_a, wp_b, wa_a, wa_b, pairs_ref, keep_ref, pass_ref, part_ref, *refs = refs
    hidden_ref, cur_ref, fol_ref = refs
    step = token_refs[0].shape[0]
    seq_place = lax.axis_index("seq")
    split_place = lax.axis_index(("head", "sub"))
    roll = (seq_place * 2 + lax.axis_index("sub")) * cols // patches
    for place, ref in enumerate(token_refs):
        rows = slice(place * step, (place + 1) * step)
        branch = own_ref[rows, :].astype(jnp.float32)
        for index, other in enumerate(other_refs):
            there = place ^ (2 * (index + 1))
            branch = branch + other[there * step : (there + 1) * step, :].astype(jnp.float32)
        hidden_ref[rows, :] = (ref[...].astype(jnp.float32) + branch).astype(jnp.bfloat16)
    keep_ref[...] = hidden_ref[:step, :]
    pass_ref[...] = hidden_ref[step : 2 * step, :]
    vit = scaled(hidden_ref[...].astype(jnp.float32), lined(gain_ref))
    scored = None
    for wp_ref, wa_ref in ((wp_a, wa_a), (wp_b, wa_b)):
        current = jnp.dot(vit, wp_ref[0], preferred_element_type=jnp.float32)
        ahead = jnp.dot(vit, wp_ref[1], preferred_element_type=jnp.float32)
        for split in range(split_count):
            for seq in range(seq_count):
                frame = (seq_place ^ seq) * split_count + (split_place ^ split)
                piece = slice((split * seq_count + seq) * cols, (split * seq_count + seq + 1) * cols)
                place = pl.ds(pl.multiple_of(frame * cols, cols), cols)
                cur_ref[place, :] = current[piece, :]
                fol_ref[place, :] = ahead[piece, :]
        embedded = cur_ref[: (frames - 1) * cols, :] + fol_ref[cols:, :]
        activated = 0.5 * embedded * (1.0 + lax.erf(embedded * (0.5**0.5)))
        pooled = jnp.sum(activated.reshape(frames - 1, cols, -1), axis=1) * (1.0 / patches)
        here = lax.dot_general(
            wa_ref[...], pooled, (((1,), (1,)), ((), ())),
            preferred_element_type=jnp.float32, precision=lax.Precision.HIGHEST,
        )
        scored = here if scored is None else scored + here
    wanted = pairs_ref.shape[1]
    part_ref[...] = jnp.zeros_like(part_ref)
    for index in range(ROLLS):
        chosen = pairs_ref[index : index + 1, :] == lax.broadcasted_iota(
            jnp.int32, (frames - 1, wanted), 0
        )
        first = index * LINES
        part_ref[first : first + scored.shape[0], :wanted] = jnp.dot(
            scored, jnp.where(chosen & (roll == index), 1.0, 0.0),
            preferred_element_type=jnp.float32, precision=lax.Precision.HIGHEST,
        )


def pack_kernel(cols, parts, kept_ref, arrived_ref, *refs):
    part_refs, block_refs = refs[:parts], refs[parts:]
    width = kept_ref.shape[1]
    total = part_refs[0][...]
    for ref in part_refs[1:]:
        total = total + ref[...]
    high = total.astype(jnp.bfloat16)
    low = (total - high.astype(jnp.float32)).astype(jnp.bfloat16)
    height, lanes = total.shape
    for block_ref in block_refs:
        block_ref[:height, width : width + lanes] = high
        block_ref[:height, width + lanes :] = low
    for lower, (first_ref, second_ref) in enumerate(
        ((arrived_ref, kept_ref), (kept_ref, arrived_ref))
    ):

        @pl.when(lax.axis_index("sub") == 1 - lower)
        def _():
            for step, block_ref in enumerate(block_refs):
                rows = slice(step * cols, (step + 1) * cols)
                block_ref[:cols, :width] = first_ref[rows, :]
                block_ref[cols:, :width] = second_ref[rows, :]


def place_kernel(seq_count, wide, *refs):
    block_refs, (hidden_ref, actions_ref) = refs[:seq_count], refs[seq_count:]
    width = hidden_ref.shape[1]
    lanes = (block_refs[0].shape[1] - width) // 2
    height = ROLLS * LINES
    total = None
    for step, ref in enumerate(block_refs):
        first = pl.multiple_of((lax.axis_index("seq") ^ step) * wide, wide)
        hidden_ref[pl.ds(first, wide), :] = ref[:, :width]
        part = ref[:height, width : width + lanes].astype(jnp.float32)
        part = part + ref[:height, width + lanes :].astype(jnp.float32)
        total = part if total is None else total + part
    outs, _, each = actions_ref.shape
    for roll in range(ROLLS):
        actions_ref[:, roll, :] = total[roll * LINES : roll * LINES + outs, :each]


def fast_shards(frames_in, attn_gain, w_qkv, w_out, vit_gain, w_pair, w_act, pair_frames):
    rows_own, width = frames_in.shape
    seq_count = lax.axis_size("seq")
    head_count = lax.axis_size("head")
    split_count = head_count * 2
    heads, triple = w_qkv.shape[1:]
    head_dim = triple // 3
    wide = rows_own // seq_count
    cols = wide // 2
    patches = rows_own // ROLLS
    vmem = pl.BlockSpec(memory_space=pltpu.VMEM)
    hbm = pl.BlockSpec(memory_space=pltpu.HBM)
    wq_own = jnp.transpose(w_qkv, (1, 2, 0)).reshape(heads * triple, width)
    wa_own = w_act.T
    small = [attn_gain.reshape(-1, 128), vit_gain.reshape(-1, 128), wa_own, pair_frames]
    cut = pl.pallas_call(
        functools.partial(cut_kernel, seq_count, len(small)),
        compiler_params=GRANT,
        in_specs=[hbm] * (1 + len(small)),
        out_specs=[vmem] * (seq_count + len(small)),
        out_shape=[pltpu.VMEM((wide, width), jnp.bfloat16)] * seq_count
        + [pltpu.VMEM(value.shape, value.dtype) for value in small],
        scratch_shapes=[pltpu.SemaphoreType.DMA((seq_count + len(small),))],
    )(off_chip(frames_in), *[off_chip(value) for value in small])
    pieces = cut[:seq_count]
    attn_gain, vit_gain, wa_own, pair_frames = cut[seq_count:]
    pieces = [pieces[0]] + [swap(pieces[step], "seq", step) for step in range(1, seq_count)]
    wq_pal = swap(wq_own, "sub", 1)
    wo_pal = swap(w_out, "sub", 1)
    wp_pal = swap(w_pair, "sub", 1)
    wa_pal = swap(wa_own, "sub", 1)
    half = pltpu.VMEM((seq_count * cols, width), jnp.bfloat16)
    mine, pals = pl.pallas_call(
        functools.partial(halve_kernel, cols),
        compiler_params=GRANT,
        in_specs=[vmem] * seq_count,
        out_specs=[vmem] * 2,
        out_shape=[half] * 2,
    )(*pieces)
    tokens = [mine] + [
        swap(pals if step & 1 else mine, ("head", "sub"), step)
        for step in range(1, split_count)
    ]
    rows = split_count * seq_count * cols
    inner = heads * head_dim
    branch = pl.pallas_call(
        functools.partial(attend_kernel, cols, heads, head_dim),
        compiler_params=GRANT,
        in_specs=[vmem] * (split_count + 1) + [hbm, vmem, hbm, vmem],
        out_specs=vmem,
        out_shape=pltpu.VMEM((rows, width), jnp.bfloat16),
        scratch_shapes=[
            pltpu.VMEM((rows, width), jnp.bfloat16),
            pltpu.VMEM((6 * inner, rows), jnp.bfloat16),
            pltpu.VMEM((2 * inner, rows), jnp.bfloat16),
            pltpu.VMEM((3 * inner, width), jnp.bfloat16),
            pltpu.VMEM((inner, width), jnp.bfloat16),
            pltpu.SemaphoreType.DMA((heads + 1,)),
        ],
    )(*tokens, attn_gain, off_chip(wq_own), wq_pal, off_chip(w_out), wo_pal)
    others = [swap(branch, "head", step) for step in range(1, head_count)]
    embed = w_pair.shape[2]
    wanted = pair_frames.shape[1]
    kept, passed, part = pl.pallas_call(
        functools.partial(
            pair_kernel, cols, F, seq_count, split_count, patches, head_count - 1
        ),
        compiler_params=GRANT,
        in_specs=[vmem] * (split_count + head_count + 6),
        out_specs=[vmem] * 3,
        out_shape=(half, half, pltpu.VMEM((ROLLS * LINES, 128), jnp.float32)),
        scratch_shapes=[
            pltpu.VMEM((rows, width), jnp.bfloat16),
            pltpu.VMEM((rows, embed), jnp.float32),
            pltpu.VMEM((rows, embed), jnp.float32),
        ],
    )(
        *tokens, branch, *others, vit_gain, on_chip(w_pair), wp_pal,
        wa_own, wa_pal, pair_frames,
    )
    arrived = swap(passed, "sub", 1)
    parts = [part] + [swap(part, ("head", "sub"), step) for step in range(1, split_count)]
    blocks = pl.pallas_call(
        functools.partial(pack_kernel, cols, split_count),
        compiler_params=GRANT,
        in_specs=[vmem] * (2 + split_count),
        out_specs=[vmem] * seq_count,
        out_shape=[pltpu.VMEM((wide, width + 256), jnp.bfloat16)] * seq_count,
    )(kept, arrived, *parts)
    blocks = [blocks[0]] + [swap(blocks[step], "seq", step) for step in range(1, seq_count)]
    hidden, actions = pl.pallas_call(
        functools.partial(place_kernel, seq_count, wide),
        compiler_params=GRANT,
        in_specs=[vmem] * seq_count,
        out_shape=(
            jax.ShapeDtypeStruct((rows_own, width), jnp.bfloat16),
            jax.ShapeDtypeStruct((w_act.shape[1], ROLLS, wanted), jnp.float32),
        ),
    )(*blocks)
    return hidden, jnp.transpose(actions, (1, 2, 0))


def shards(frames_in, attn_gain, w_qkv, w_out, vit_gain, w_pair, w_act, pair_frames):
    seq_count = lax.axis_size("seq")
    head_count = lax.axis_size("head")
    rows_own = frames_in.shape[0]
    powers = all(count & (count - 1) == 0 for count in (seq_count, head_count))
    one_frame = seq_count * head_count * lax.axis_size("sub") == F
    tiled = rows_own % (seq_count * 16) == 0 and lax.axis_size("sub") == 2
    tiled = tiled and rows_own // seq_count >= ROLLS * LINES
    tiled = tiled and pair_frames.shape[1] <= 128 and w_act.shape[1] <= LINES
    tiled = tiled and frames_in.shape[1] % 128 == 0
    chosen = fast_shards if powers and one_frame and tiled else general_shards
    return chosen(frames_in, attn_gain, w_qkv, w_out, vit_gain, w_pair, w_act, pair_frames)


def solution(mesh):
    in_specs = (
        P(("groups", "seq", "head", "sub"), None),
        P(),
        P(None, ("head", "sub"), None),
        P(("head", "sub"), None),
        P(),
        P(None, None, ("head", "sub")),
        P(("head", "sub"), None),
        P("groups", None),
    )
    out_specs = (P(("groups", "seq", "head", "sub"), None), P("groups", None, None))
    return jax.shard_map(shards, mesh=mesh, in_specs=in_specs, out_specs=out_specs, check_vma=False)
```

```python
import functools

import jax
import jax.numpy as jnp
from jax import lax
from jax.experimental import pallas as pl
from jax.experimental.pallas import tpu as pltpu
from jax.sharding import PartitionSpec as P


F = 16
ROLLS = 2
EPS = 1e-06
LINES = 8


def from_behind(value, axis, steps):
    count = lax.axis_size(axis)
    leading, last = (max(0, -steps), min(count, count - steps))
    return lax.ppermute(value, axis, [(source, source + steps) for source in range(leading, last)])


def normalize(values_in, gain_vec):
    floats = values_in.astype(jnp.float32)
    mean_sq = jnp.mean(floats * floats, axis=-1, keepdims=True)
    return (floats * lax.rsqrt(mean_sq + 1e-06) * gain_vec).astype(jnp.bfloat16)


def general_shards(frames_in, attn_gain, w_qkv, w_out, vit_gain, w_pair, w_act, pair_frames):
    rows_own = frames_in.shape[0]
    model_width = frames_in.shape[1]
    seq_count = lax.axis_size("seq")
    split_count = lax.axis_size(("head", "sub"))
    block_rows = rows_own * split_count
    total_cols = block_rows * seq_count // F
    frames_local = max(1, F // seq_count)
    cols_local = block_rows // frames_local
    frame_step = max(1, seq_count // F)
    heads_local = w_qkv.shape[1]
    triple_dim = w_qkv.shape[2]
    head_dim = triple_dim // 3
    qkv_matrix = w_qkv.reshape(model_width, heads_local * triple_dim)
    normed = lax.all_gather(normalize(frames_in, attn_gain), ("head", "sub"), axis=0, tiled=True)
    qkv_rows = jnp.dot(normed, qkv_matrix, preferred_element_type=jnp.float32).astype(jnp.bfloat16)
    qkv_rows = qkv_rows.reshape(
        frames_local, seq_count, cols_local // seq_count, heads_local, triple_dim
    )
    columns = lax.all_to_all(qkv_rows, "seq", split_axis=1, concat_axis=0, tiled=True)
    item_count = columns.shape[2]
    by_frame = columns.reshape(F, -1, heads_local, triple_dim)
    queries = by_frame[..., :head_dim]
    key_part = by_frame[..., head_dim : 2 * head_dim]
    value_part = by_frame[..., 2 * head_dim :]
    scores = jnp.einsum(
        "fchd,gchd->chfg", queries, key_part, preferred_element_type=jnp.float32
    ) * head_dim ** (-0.5)
    row_peak = jnp.max(scores, axis=-1, keepdims=True)
    weights = jnp.exp(scores - row_peak)
    weights = (weights / jnp.sum(weights, axis=-1, keepdims=True)).astype(jnp.bfloat16)
    mixed_out = jnp.einsum(
        "chfg,gchd->fchd", weights, value_part, preferred_element_type=jnp.float32
    ).astype(jnp.bfloat16)
    mixed_out = mixed_out.reshape(seq_count * frames_local, 1, item_count, heads_local * head_dim)
    attended = lax.all_to_all(mixed_out, "seq", split_axis=0, concat_axis=1, tiled=True)
    attended = attended.reshape(block_rows, heads_local * head_dim)
    branch_sum = lax.psum_scatter(
        jnp.dot(attended, w_out, preferred_element_type=jnp.float32).astype(jnp.bfloat16),
        ("head", "sub"),
        scatter_dimension=0,
        tiled=True,
    ).astype(jnp.float32)
    hidden = (frames_in.astype(jnp.float32) + branch_sum).astype(jnp.bfloat16)
    vit_own = normalize(hidden, vit_gain)
    vit_rows = lax.all_gather(vit_own, ("head", "sub"), axis=0, tiled=True)
    current = jnp.dot(vit_rows, w_pair[0], preferred_element_type=jnp.float32)
    ahead_proj = jnp.dot(vit_rows, w_pair[1], preferred_element_type=jnp.float32)
    ahead_proj = ahead_proj.reshape(frames_local, cols_local, -1)
    arrived = from_behind(ahead_proj[:1].astype(jnp.bfloat16), "seq", -frame_step).astype(
        jnp.float32
    )
    following = jnp.concatenate([ahead_proj[1:], arrived], axis=0).reshape(block_rows, -1)
    embedded = current + following
    activated = jax.nn.gelu(embedded, approximate=False).reshape(frames_local, cols_local, -1)
    seq_index = lax.axis_index("seq")
    first_token = seq_index * block_rows
    frame_first = first_token // total_cols
    col_first = first_token % total_cols
    patches = total_cols // ROLLS
    roll_ids = (col_first + jnp.arange(cols_local, dtype=jnp.int32)) // patches
    member = (roll_ids[None, :] == jnp.arange(ROLLS, dtype=jnp.int32)[:, None]).astype(
        jnp.float32
    ) / patches
    pooled = jnp.einsum("rp,fpe->fre", member, activated, precision=lax.Precision.HIGHEST)
    scored = jnp.einsum("fre,ea->fra", pooled, w_act, precision=lax.Precision.HIGHEST)
    frame_ids = frame_first + jnp.arange(frames_local, dtype=jnp.int32)
    selector = (pair_frames[:, :, None] == frame_ids[None, None, :]).astype(jnp.float32)
    partial_value = jnp.einsum("rjf,fra->rja", selector, scored, precision=lax.Precision.HIGHEST)
    actions = lax.psum(partial_value, ("seq", "head", "sub"))
    return (hidden, actions)


GRANT = pltpu.CompilerParams(vmem_limit_bytes=12 * 1024 * 1024)


def on_chip(value):
    return pltpu.with_memory_space_constraint(value, pltpu.VMEM)


def off_chip(value):
    return pltpu.with_memory_space_constraint(value, pltpu.HBM)


def swap(value, axis, mask):
    count = lax.axis_size(axis)
    pairs = [(source, source ^ mask) for source in range(count)]
    return on_chip(lax.ppermute(value, axis, pairs))


def lined(gain_ref):
    return jnp.concatenate([gain_ref[row : row + 1, :] for row in range(gain_ref.shape[0])], axis=1)


def scaled(rows, gain_row):
    mean_sq = jnp.mean(rows * rows, axis=-1, keepdims=True)
    return (rows * lax.rsqrt(mean_sq + EPS) * gain_row).astype(jnp.bfloat16)


def cut_kernel(seq_count, small, tokens_ref, *refs):
    small_refs, out_refs, sems = refs[:small], refs[small:-1], refs[-1]
    wide = out_refs[0].shape[0]
    place = lax.axis_index("seq")
    copies = []
    for step, out_ref in enumerate(out_refs[:seq_count]):
        first = pl.multiple_of((place ^ step) * wide, wide)
        source = tokens_ref.at[pl.ds(first, wide), :]
        copies.append(pltpu.make_async_copy(source, out_ref, sems.at[step]))
    for source, out_ref in zip(small_refs, out_refs[seq_count:]):
        copies.append(pltpu.make_async_copy(source, out_ref, sems.at[len(copies)]))
    for copy in copies:
        copy.start()
    for copy in copies:
        copy.wait()


def halve_kernel(cols, *refs):
    *piece_refs, mine_ref, pals_ref = refs
    for lower, (first_ref, second_ref) in enumerate(((pals_ref, mine_ref), (mine_ref, pals_ref))):

        @pl.when(lax.axis_index("sub") == 1 - lower)
        def _():
            for step, ref in enumerate(piece_refs):
                rows = slice(step * cols, (step + 1) * cols)
                first_ref[rows, :] = ref[:cols, :]
                second_ref[rows, :] = ref[cols:, :]


def aligned(value, step):
    return value if isinstance(value, int) else pl.multiple_of(value, step)


def each(count, body):
    lax.fori_loop(0, count, lambda index, carry: (body(index), carry)[1], 0)


def attend_kernel(cols, heads, head_dim, *refs):
    *token_refs, gain_ref, wq_far, wq_pal, wo_far, wo_pal, out_ref = refs[:-6]
    normed_ref, qkv_ref, mixed_ref, wq_own, wo_own, sems = refs[-6:]
    triple = 3 * head_dim
    inner = heads * head_dim
    group = 2 if heads % 2 == 0 else 1
    chunk = group * triple

    def fetch(index):
        piece = pl.ds(aligned(index * chunk, chunk), chunk)
        return pltpu.make_async_copy(wq_far.at[piece, :], wq_own.at[piece, :], sems.at[index])

    for index in range(heads // group):
        fetch(index).start()
    fetch_out = pltpu.make_async_copy(wo_far, wo_own, sems.at[heads // group])
    fetch_out.start()
    gain_row = lined(gain_ref)
    first = 0
    for ref in token_refs:
        normed_ref[first : first + ref.shape[0], :] = scaled(
            ref[...].astype(jnp.float32), gain_row
        )
        first += ref.shape[0]
    rows = normed_ref.shape[0]

    def project(wq_ref, source, size, target):
        qkv_ref[pl.ds(aligned(target, head_dim), size), :] = lax.dot_general(
            wq_ref[pl.ds(aligned(source, size), size), :], normed_ref[...],
            (((1,), (1,)), ((), ())), preferred_element_type=jnp.float32,
        ).astype(jnp.bfloat16)

    large = heads * triple // group

    def project_pal(index):
        project(wq_pal, index * large, large, index * large)

    def project_own(index):
        fetch(index).wait()
        project(wq_own, index * chunk, chunk, heads * triple + index * chunk)

    each(group, project_pal)
    each(heads // group, project_own)
    left = lax.broadcasted_iota(jnp.int32, (rows, rows), 0) % cols
    right = lax.broadcasted_iota(jnp.int32, (rows, rows), 1) % cols
    same = left == right
    for head in range(2 * heads):
        base = head * triple
        query = qkv_ref[base : base + head_dim, :]
        key = qkv_ref[base + head_dim : base + 2 * head_dim, :]
        val = qkv_ref[base + 2 * head_dim : base + triple, :]
        scores = lax.dot_general(
            key, query, (((0,), (0,)), ((), ())), preferred_element_type=jnp.float32
        ) * head_dim ** (-0.5)
        scores = jnp.where(same, scores, -jnp.inf)
        weights = jnp.exp(scores - jnp.max(scores, axis=0, keepdims=True))
        weights = weights * (1.0 / jnp.sum(weights, axis=0, keepdims=True))
        mixed_ref[head * head_dim : (head + 1) * head_dim, :] = jnp.dot(
            val, weights.astype(jnp.bfloat16), preferred_element_type=jnp.float32
        ).astype(jnp.bfloat16)
    fetch_out.wait()
    total = None
    for index, wo_ref in enumerate((wo_pal, wo_own)):
        product = lax.dot_general(
            mixed_ref[index * inner : (index + 1) * inner, :], wo_ref[...],
            (((0,), (0,)), ((), ())), preferred_element_type=jnp.float32,
        ).astype(jnp.bfloat16).astype(jnp.float32)
        total = product if total is None else total + product
    out_ref[...] = total.astype(jnp.bfloat16)


def pair_kernel(cols, frames, order, split_count, patches, others, *refs):
    batches = 2 * split_count
    token_refs, refs = refs[:batches], refs[batches:]
    own_ref, refs = refs[0], refs[1:]
    other_refs, refs = refs[:others], refs[others:]
    gain_ref, wp_a, wp_b, wa_a, wa_b, pairs_ref, keep_ref, pass_ref, part_ref, *refs = refs
    hidden_ref, cur_ref, fol_ref = refs
    seq_count = len(order)
    step = seq_count * cols
    seq_place = lax.axis_index("seq")
    split_place = lax.axis_index(("head", "sub"))
    roll = (seq_place * 2 + lax.axis_index("sub")) * cols // patches
    for place in range(split_count):
        first = place * step
        for ref in token_refs[2 * place : 2 * place + 2]:
            height = ref.shape[0]
            rows = slice(first, first + height)
            branch = own_ref[rows, :].astype(jnp.float32)
            for index, other in enumerate(other_refs):
                there = first + ((place ^ (2 * (index + 1))) - place) * step
                branch = branch + other[there : there + height, :].astype(jnp.float32)
            hidden_ref[rows, :] = (ref[...].astype(jnp.float32) + branch).astype(jnp.bfloat16)
            first += height
    keep_ref[...] = hidden_ref[:step, :]
    pass_ref[...] = hidden_ref[step : 2 * step, :]
    vit = scaled(hidden_ref[...].astype(jnp.float32), lined(gain_ref))
    scored = None
    for wp_ref, wa_ref in ((wp_a, wa_a), (wp_b, wa_b)):
        current = jnp.dot(vit, wp_ref[0], preferred_element_type=jnp.float32)
        ahead = jnp.dot(vit, wp_ref[1], preferred_element_type=jnp.float32)
        for split in range(split_count):
            for index, seq in enumerate(order):
                frame = (seq_place ^ seq) * split_count + (split_place ^ split)
                first = (split * seq_count + index) * cols
                piece = slice(first, first + cols)
                place = pl.ds(pl.multiple_of(frame * cols, cols), cols)
                cur_ref[place, :] = current[piece, :]
                fol_ref[place, :] = ahead[piece, :]
        embedded = cur_ref[: (frames - 1) * cols, :] + fol_ref[cols:, :]
        activated = 0.5 * embedded * (1.0 + lax.erf(embedded * (0.5**0.5)))
        pooled = jnp.sum(activated.reshape(frames - 1, cols, -1), axis=1) * (1.0 / patches)
        here = lax.dot_general(
            wa_ref[...], pooled, (((1,), (1,)), ((), ())),
            preferred_element_type=jnp.float32, precision=lax.Precision.HIGHEST,
        )
        scored = here if scored is None else scored + here
    wanted = pairs_ref.shape[1]
    part_ref[...] = jnp.zeros_like(part_ref)
    for index in range(ROLLS):
        chosen = pairs_ref[index : index + 1, :] == lax.broadcasted_iota(
            jnp.int32, (frames - 1, wanted), 0
        )
        first = index * LINES
        part_ref[first : first + scored.shape[0], :wanted] = jnp.dot(
            scored, jnp.where(chosen & (roll == index), 1.0, 0.0),
            preferred_element_type=jnp.float32, precision=lax.Precision.HIGHEST,
        )


def pack_kernel(cols, order, parts, kept_ref, arrived_ref, *refs):
    part_refs, block_refs = refs[:parts], refs[parts:]
    width = kept_ref.shape[1]
    total = part_refs[0][...]
    for ref in part_refs[1:]:
        total = total + ref[...]
    high = total.astype(jnp.bfloat16)
    low = (total - high.astype(jnp.float32)).astype(jnp.bfloat16)
    height, lanes = total.shape
    for block_ref in block_refs:
        block_ref[:height, width : width + lanes] = high
        block_ref[:height, width + lanes :] = low
    for lower, (first_ref, second_ref) in enumerate(
        ((arrived_ref, kept_ref), (kept_ref, arrived_ref))
    ):

        @pl.when(lax.axis_index("sub") == 1 - lower)
        def _():
            for index, step in enumerate(order):
                block_ref = block_refs[step]
                rows = slice(index * cols, (index + 1) * cols)
                block_ref[:cols, :width] = first_ref[rows, :]
                block_ref[cols:, :width] = second_ref[rows, :]


def place_kernel(seq_count, wide, *refs):
    block_refs, (hidden_ref, actions_ref) = refs[:seq_count], refs[seq_count:]
    width = hidden_ref.shape[1]
    lanes = (block_refs[0].shape[1] - width) // 2
    height = ROLLS * LINES
    total = None
    for step, ref in enumerate(block_refs):
        first = pl.multiple_of((lax.axis_index("seq") ^ step) * wide, wide)
        hidden_ref[pl.ds(first, wide), :] = ref[:, :width]
        part = ref[:height, width : width + lanes].astype(jnp.float32)
        part = part + ref[:height, width + lanes :].astype(jnp.float32)
        total = part if total is None else total + part
    outs, _, each = actions_ref.shape
    for roll in range(ROLLS):
        actions_ref[:, roll, :] = total[roll * LINES : roll * LINES + outs, :each]


def fast_shards(frames_in, attn_gain, w_qkv, w_out, vit_gain, w_pair, w_act, pair_frames):
    rows_own, width = frames_in.shape
    seq_count = lax.axis_size("seq")
    head_count = lax.axis_size("head")
    split_count = head_count * 2
    heads, triple = w_qkv.shape[1:]
    head_dim = triple // 3
    wide = rows_own // seq_count
    cols = wide // 2
    patches = rows_own // ROLLS
    vmem = pl.BlockSpec(memory_space=pltpu.VMEM)
    hbm = pl.BlockSpec(memory_space=pltpu.HBM)
    wq_own = jnp.transpose(w_qkv, (1, 2, 0)).reshape(heads * triple, width)
    wa_own = w_act.T
    small = [attn_gain.reshape(-1, 128), vit_gain.reshape(-1, 128), wa_own, pair_frames]
    cut = pl.pallas_call(
        functools.partial(cut_kernel, seq_count, len(small)),
        compiler_params=GRANT,
        in_specs=[hbm] * (1 + len(small)),
        out_specs=[vmem] * (seq_count + len(small)),
        out_shape=[pltpu.VMEM((wide, width), jnp.bfloat16)] * seq_count
        + [pltpu.VMEM(value.shape, value.dtype) for value in small],
        scratch_shapes=[pltpu.SemaphoreType.DMA((seq_count + len(small),))],
    )(off_chip(frames_in), *[off_chip(value) for value in small])
    pieces = cut[:seq_count]
    attn_gain, vit_gain, wa_own, pair_frames = cut[seq_count:]
    cut_pieces = pieces
    pieces = [cut_pieces[0]]
    for step in range(1, seq_count):
        pieces.append(swap(cut_pieces[step], "seq", step))
    wq_pal = swap(wq_own, "sub", 1)
    wo_pal = swap(w_out, "sub", 1)
    wp_pal = swap(w_pair, "sub", 1)
    wa_pal = swap(wa_own, "sub", 1)
    half = pltpu.VMEM((seq_count * cols, width), jnp.bfloat16)
    middle = seq_count // 2
    early = (0, middle) if seq_count > 2 else (0,)
    late = tuple(step for step in range(1, seq_count) if step not in early)
    order = early + late
    batches = []
    for steps in (early, late):
        mine, pals = pl.pallas_call(
            functools.partial(halve_kernel, cols),
            compiler_params=GRANT,
            in_specs=[vmem] * len(steps),
            out_specs=[vmem] * 2,
            out_shape=[pltpu.VMEM((len(steps) * cols, width), jnp.bfloat16)] * 2,
        )(*[pieces[step] for step in steps])
        batch = [mine]
        for step in range(1, split_count):
            batch.append(swap(pals if step & 1 else mine, ("head", "sub"), step))
        batches.append(batch)
    tokens = [batch[step] for step in range(split_count) for batch in batches]
    rows = split_count * seq_count * cols
    inner = heads * head_dim
    branch = pl.pallas_call(
        functools.partial(attend_kernel, cols, heads, head_dim),
        compiler_params=GRANT,
        in_specs=[vmem] * (2 * split_count + 1) + [hbm, vmem, hbm, vmem],
        out_specs=vmem,
        out_shape=pltpu.VMEM((rows, width), jnp.bfloat16),
        scratch_shapes=[
            pltpu.VMEM((rows, width), jnp.bfloat16),
            pltpu.VMEM((6 * inner, rows), jnp.bfloat16),
            pltpu.VMEM((2 * inner, rows), jnp.bfloat16),
            pltpu.VMEM((3 * inner, width), jnp.bfloat16),
            pltpu.VMEM((inner, width), jnp.bfloat16),
            pltpu.SemaphoreType.DMA((heads + 1,)),
        ],
    )(*tokens, attn_gain, off_chip(wq_own), wq_pal, off_chip(w_out), wo_pal)
    others = [swap(branch, "head", step) for step in range(1, head_count)]
    embed = w_pair.shape[2]
    wanted = pair_frames.shape[1]
    kept, passed, part = pl.pallas_call(
        functools.partial(
            pair_kernel, cols, F, order, split_count, patches, head_count - 1
        ),
        compiler_params=GRANT,
        in_specs=[vmem] * (2 * split_count + head_count + 6),
        out_specs=[vmem] * 3,
        out_shape=(half, half, pltpu.VMEM((ROLLS * LINES, 128), jnp.float32)),
        scratch_shapes=[
            pltpu.VMEM((rows, width), jnp.bfloat16),
            pltpu.VMEM((rows, embed), jnp.float32),
            pltpu.VMEM((rows, embed), jnp.float32),
        ],
    )(
        *tokens, branch, *others, vit_gain, on_chip(w_pair), wp_pal,
        wa_own, wa_pal, pair_frames,
    )
    arrived = swap(passed, "sub", 1)
    parts = [part]
    for step in range(1, split_count):
        parts.append(swap(part, ("head", "sub"), step))
    blocks = pl.pallas_call(
        functools.partial(pack_kernel, cols, order, split_count),
        compiler_params=GRANT,
        in_specs=[vmem] * (2 + split_count),
        out_specs=[vmem] * seq_count,
        out_shape=[pltpu.VMEM((wide, width + 256), jnp.bfloat16)] * seq_count,
    )(kept, arrived, *parts)
    cut_blocks = blocks
    blocks = [cut_blocks[0]]
    for step in range(1, seq_count):
        blocks.append(swap(cut_blocks[step], "seq", step))
    hidden, actions = pl.pallas_call(
        functools.partial(place_kernel, seq_count, wide),
        compiler_params=GRANT,
        in_specs=[vmem] * seq_count,
        out_shape=(
            jax.ShapeDtypeStruct((rows_own, width), jnp.bfloat16),
            jax.ShapeDtypeStruct((w_act.shape[1], ROLLS, wanted), jnp.float32),
        ),
    )(*blocks)
    return hidden, jnp.transpose(actions, (1, 2, 0))


def shards(frames_in, attn_gain, w_qkv, w_out, vit_gain, w_pair, w_act, pair_frames):
    seq_count = lax.axis_size("seq")
    head_count = lax.axis_size("head")
    rows_own = frames_in.shape[0]
    powers = all(count & (count - 1) == 0 for count in (seq_count, head_count))
    one_frame = seq_count * head_count * lax.axis_size("sub") == F
    tiled = rows_own % (seq_count * 16) == 0 and lax.axis_size("sub") == 2
    tiled = tiled and rows_own // seq_count >= ROLLS * LINES
    tiled = tiled and pair_frames.shape[1] <= 128 and w_act.shape[1] <= LINES
    tiled = tiled and frames_in.shape[1] % 128 == 0
    chosen = fast_shards if powers and one_frame and tiled else general_shards
    return chosen(frames_in, attn_gain, w_qkv, w_out, vit_gain, w_pair, w_act, pair_frames)


def solution(mesh):
    in_specs = (
        P(("groups", "seq", "head", "sub"), None),
        P(),
        P(None, ("head", "sub"), None),
        P(("head", "sub"), None),
        P(),
        P(None, None, ("head", "sub")),
        P(("head", "sub"), None),
        P("groups", None),
    )
    out_specs = (P(("groups", "seq", "head", "sub"), None), P("groups", None, None))
    return jax.shard_map(shards, mesh=mesh, in_specs=in_specs, out_specs=out_specs, check_vma=False)
```

```python
import functools

import jax
import jax.numpy as jnp
from jax import lax
from jax.experimental import pallas as pl
from jax.experimental.pallas import tpu as pltpu
from jax.sharding import PartitionSpec as P


F = 16
ROLLS = 2
EPS = 1e-06
LINES = 8


def from_behind(value, axis, steps):
    count = lax.axis_size(axis)
    leading, last = (max(0, -steps), min(count, count - steps))
    return lax.ppermute(value, axis, [(source, source + steps) for source in range(leading, last)])


def normalize(values_in, gain_vec):
    floats = values_in.astype(jnp.float32)
    mean_sq = jnp.mean(floats * floats, axis=-1, keepdims=True)
    return (floats * lax.rsqrt(mean_sq + 1e-06) * gain_vec).astype(jnp.bfloat16)


def general_shards(frames_in, attn_gain, w_qkv, w_out, vit_gain, w_pair, w_act, pair_frames):
    rows_own = frames_in.shape[0]
    model_width = frames_in.shape[1]
    seq_count = lax.axis_size("seq")
    split_count = lax.axis_size(("head", "sub"))
    block_rows = rows_own * split_count
    total_cols = block_rows * seq_count // F
    frames_local = max(1, F // seq_count)
    cols_local = block_rows // frames_local
    frame_step = max(1, seq_count // F)
    heads_local = w_qkv.shape[1]
    triple_dim = w_qkv.shape[2]
    head_dim = triple_dim // 3
    qkv_matrix = w_qkv.reshape(model_width, heads_local * triple_dim)
    normed = lax.all_gather(normalize(frames_in, attn_gain), ("head", "sub"), axis=0, tiled=True)
    qkv_rows = jnp.dot(normed, qkv_matrix, preferred_element_type=jnp.float32).astype(jnp.bfloat16)
    qkv_rows = qkv_rows.reshape(
        frames_local, seq_count, cols_local // seq_count, heads_local, triple_dim
    )
    columns = lax.all_to_all(qkv_rows, "seq", split_axis=1, concat_axis=0, tiled=True)
    item_count = columns.shape[2]
    by_frame = columns.reshape(F, -1, heads_local, triple_dim)
    queries = by_frame[..., :head_dim]
    key_part = by_frame[..., head_dim : 2 * head_dim]
    value_part = by_frame[..., 2 * head_dim :]
    scores = jnp.einsum(
        "fchd,gchd->chfg", queries, key_part, preferred_element_type=jnp.float32
    ) * head_dim ** (-0.5)
    row_peak = jnp.max(scores, axis=-1, keepdims=True)
    weights = jnp.exp(scores - row_peak)
    weights = (weights / jnp.sum(weights, axis=-1, keepdims=True)).astype(jnp.bfloat16)
    mixed_out = jnp.einsum(
        "chfg,gchd->fchd", weights, value_part, preferred_element_type=jnp.float32
    ).astype(jnp.bfloat16)
    mixed_out = mixed_out.reshape(seq_count * frames_local, 1, item_count, heads_local * head_dim)
    attended = lax.all_to_all(mixed_out, "seq", split_axis=0, concat_axis=1, tiled=True)
    attended = attended.reshape(block_rows, heads_local * head_dim)
    branch_sum = lax.psum_scatter(
        jnp.dot(attended, w_out, preferred_element_type=jnp.float32).astype(jnp.bfloat16),
        ("head", "sub"),
        scatter_dimension=0,
        tiled=True,
    ).astype(jnp.float32)
    hidden = (frames_in.astype(jnp.float32) + branch_sum).astype(jnp.bfloat16)
    vit_own = normalize(hidden, vit_gain)
    vit_rows = lax.all_gather(vit_own, ("head", "sub"), axis=0, tiled=True)
    current = jnp.dot(vit_rows, w_pair[0], preferred_element_type=jnp.float32)
    ahead_proj = jnp.dot(vit_rows, w_pair[1], preferred_element_type=jnp.float32)
    ahead_proj = ahead_proj.reshape(frames_local, cols_local, -1)
    arrived = from_behind(ahead_proj[:1].astype(jnp.bfloat16), "seq", -frame_step).astype(
        jnp.float32
    )
    following = jnp.concatenate([ahead_proj[1:], arrived], axis=0).reshape(block_rows, -1)
    embedded = current + following
    activated = jax.nn.gelu(embedded, approximate=False).reshape(frames_local, cols_local, -1)
    seq_index = lax.axis_index("seq")
    first_token = seq_index * block_rows
    frame_first = first_token // total_cols
    col_first = first_token % total_cols
    patches = total_cols // ROLLS
    roll_ids = (col_first + jnp.arange(cols_local, dtype=jnp.int32)) // patches
    member = (roll_ids[None, :] == jnp.arange(ROLLS, dtype=jnp.int32)[:, None]).astype(
        jnp.float32
    ) / patches
    pooled = jnp.einsum("rp,fpe->fre", member, activated, precision=lax.Precision.HIGHEST)
    scored = jnp.einsum("fre,ea->fra", pooled, w_act, precision=lax.Precision.HIGHEST)
    frame_ids = frame_first + jnp.arange(frames_local, dtype=jnp.int32)
    selector = (pair_frames[:, :, None] == frame_ids[None, None, :]).astype(jnp.float32)
    partial_value = jnp.einsum("rjf,fra->rja", selector, scored, precision=lax.Precision.HIGHEST)
    actions = lax.psum(partial_value, ("seq", "head", "sub"))
    return (hidden, actions)


GRANT = pltpu.CompilerParams(vmem_limit_bytes=12 * 1024 * 1024)


def on_chip(value):
    return pltpu.with_memory_space_constraint(value, pltpu.VMEM)


def off_chip(value):
    return pltpu.with_memory_space_constraint(value, pltpu.HBM)


def swap(value, axis, mask):
    count = lax.axis_size(axis)
    pairs = [(source, source ^ mask) for source in range(count)]
    return on_chip(lax.ppermute(value, axis, pairs))


def lined(gain_ref):
    return jnp.concatenate([gain_ref[row : row + 1, :] for row in range(gain_ref.shape[0])], axis=1)


def scaled(rows, gain_row):
    mean_sq = jnp.mean(rows * rows, axis=-1, keepdims=True)
    return (rows * lax.rsqrt(mean_sq + EPS) * gain_row).astype(jnp.bfloat16)


def cut_kernel(seq_count, small, tokens_ref, *refs):
    small_refs, out_refs, sems = refs[:small], refs[small:-1], refs[-1]
    wide = out_refs[0].shape[0]
    place = lax.axis_index("seq")
    copies = []
    for step, out_ref in enumerate(out_refs[:seq_count]):
        first = pl.multiple_of((place ^ step) * wide, wide)
        source = tokens_ref.at[pl.ds(first, wide), :]
        copies.append(pltpu.make_async_copy(source, out_ref, sems.at[step]))
    for source, out_ref in zip(small_refs, out_refs[seq_count:]):
        copies.append(pltpu.make_async_copy(source, out_ref, sems.at[len(copies)]))
    for copy in copies:
        copy.start()
    for copy in copies:
        copy.wait()


def halve_kernel(cols, *refs):
    *piece_refs, mine_ref, pals_ref = refs
    for lower, (first_ref, second_ref) in enumerate(((pals_ref, mine_ref), (mine_ref, pals_ref))):

        @pl.when(lax.axis_index("sub") == 1 - lower)
        def _():
            for step, ref in enumerate(piece_refs):
                rows = slice(step * cols, (step + 1) * cols)
                first_ref[rows, :] = ref[:cols, :]
                second_ref[rows, :] = ref[cols:, :]


def aligned(value, step):
    return value if isinstance(value, int) else pl.multiple_of(value, step)


def each(count, body):
    lax.fori_loop(0, count, lambda index, carry: (body(index), carry)[1], 0)


def load_kernel(*refs):
    *refs, sems = refs
    half = len(refs) // 2
    copies = [
        pltpu.make_async_copy(refs[index], refs[half + index], sems.at[index])
        for index in range(half)
    ]
    for copy in copies:
        copy.start()
    for copy in copies:
        copy.wait()


def attend_kernel(cols, heads, head_dim, *refs):
    *token_refs, gain_ref, wq_own, wq_pal, wo_own, wo_pal, out_ref = refs[:-3]
    normed_ref, qkv_ref, mixed_ref = refs[-3:]
    triple = 3 * head_dim
    inner = heads * head_dim
    group = 2 if heads % 2 == 0 else 1
    gain_row = lined(gain_ref)
    first = 0
    for ref in token_refs:
        normed_ref[first : first + ref.shape[0], :] = scaled(
            ref[...].astype(jnp.float32), gain_row
        )
        first += ref.shape[0]
    rows = normed_ref.shape[0]

    def project(wq_ref, source, size, target):
        qkv_ref[pl.ds(aligned(target, head_dim), size), :] = lax.dot_general(
            wq_ref[pl.ds(aligned(source, size), size), :], normed_ref[...],
            (((1,), (1,)), ((), ())), preferred_element_type=jnp.float32,
        ).astype(jnp.bfloat16)

    large = heads * triple // group

    def project_both(index):
        project(wq_pal, index * large, large, index * large)
        project(wq_own, index * large, large, heads * triple + index * large)

    each(group, project_both)
    left = lax.broadcasted_iota(jnp.int32, (rows, rows), 0) % cols
    right = lax.broadcasted_iota(jnp.int32, (rows, rows), 1) % cols
    same = left == right
    for head in range(2 * heads):
        base = head * triple
        query = qkv_ref[base : base + head_dim, :]
        key = qkv_ref[base + head_dim : base + 2 * head_dim, :]
        val = qkv_ref[base + 2 * head_dim : base + triple, :]
        scores = lax.dot_general(
            key, query, (((0,), (0,)), ((), ())), preferred_element_type=jnp.float32
        ) * head_dim ** (-0.5)
        scores = jnp.where(same, scores, -jnp.inf)
        weights = jnp.exp(scores - jnp.max(scores, axis=0, keepdims=True))
        weights = weights * (1.0 / jnp.sum(weights, axis=0, keepdims=True))
        mixed_ref[head * head_dim : (head + 1) * head_dim, :] = jnp.dot(
            val, weights.astype(jnp.bfloat16), preferred_element_type=jnp.float32
        ).astype(jnp.bfloat16)
    total = None
    for index, wo_ref in enumerate((wo_pal, wo_own)):
        product = lax.dot_general(
            mixed_ref[index * inner : (index + 1) * inner, :], wo_ref[...],
            (((0,), (0,)), ((), ())), preferred_element_type=jnp.float32,
        ).astype(jnp.bfloat16).astype(jnp.float32)
        total = product if total is None else total + product
    out_ref[...] = total.astype(jnp.bfloat16)


def pair_kernel(cols, frames, order, split_count, patches, others, *refs):
    batches = 2 * split_count
    token_refs, refs = refs[:batches], refs[batches:]
    own_ref, refs = refs[0], refs[1:]
    other_refs, refs = refs[:others], refs[others:]
    gain_ref, wp_a, wp_b, wa_a, wa_b, pairs_ref, keep_ref, pass_ref, part_ref, *refs = refs
    hidden_ref, cur_ref, fol_ref = refs
    seq_count = len(order)
    step = seq_count * cols
    seq_place = lax.axis_index("seq")
    split_place = lax.axis_index(("head", "sub"))
    roll = (seq_place * 2 + lax.axis_index("sub")) * cols // patches
    for place in range(split_count):
        first = place * step
        for ref in token_refs[2 * place : 2 * place + 2]:
            height = ref.shape[0]
            rows = slice(first, first + height)
            branch = own_ref[rows, :].astype(jnp.float32)
            for index, other in enumerate(other_refs):
                there = first + ((place ^ (2 * (index + 1))) - place) * step
                branch = branch + other[there : there + height, :].astype(jnp.float32)
            hidden_ref[rows, :] = (ref[...].astype(jnp.float32) + branch).astype(jnp.bfloat16)
            first += height
    keep_ref[...] = hidden_ref[:step, :]
    pass_ref[...] = hidden_ref[step : 2 * step, :]
    vit = scaled(hidden_ref[...].astype(jnp.float32), lined(gain_ref))
    scored = None
    for wp_ref, wa_ref in ((wp_a, wa_a), (wp_b, wa_b)):
        current = jnp.dot(vit, wp_ref[0], preferred_element_type=jnp.float32)
        ahead = jnp.dot(vit, wp_ref[1], preferred_element_type=jnp.float32)
        for split in range(split_count):
            for index, seq in enumerate(order):
                frame = (seq_place ^ seq) * split_count + (split_place ^ split)
                first = (split * seq_count + index) * cols
                piece = slice(first, first + cols)
                place = pl.ds(pl.multiple_of(frame * cols, cols), cols)
                cur_ref[place, :] = current[piece, :]
                fol_ref[place, :] = ahead[piece, :]
        embedded = cur_ref[: (frames - 1) * cols, :] + fol_ref[cols:, :]
        activated = 0.5 * embedded * (1.0 + lax.erf(embedded * (0.5**0.5)))
        pooled = jnp.sum(activated.reshape(frames - 1, cols, -1), axis=1) * (1.0 / patches)
        here = lax.dot_general(
            wa_ref[...], pooled, (((1,), (1,)), ((), ())),
            preferred_element_type=jnp.float32, precision=lax.Precision.HIGHEST,
        )
        scored = here if scored is None else scored + here
    wanted = pairs_ref.shape[1]
    part_ref[...] = jnp.zeros_like(part_ref)
    for index in range(ROLLS):
        chosen = pairs_ref[index : index + 1, :] == lax.broadcasted_iota(
            jnp.int32, (frames - 1, wanted), 0
        )
        first = index * LINES
        part_ref[first : first + scored.shape[0], :wanted] = jnp.dot(
            scored, jnp.where(chosen & (roll == index), 1.0, 0.0),
            preferred_element_type=jnp.float32, precision=lax.Precision.HIGHEST,
        )


def pack_kernel(cols, order, parts, kept_ref, arrived_ref, *refs):
    part_refs, block_refs = refs[:parts], refs[parts:]
    width = kept_ref.shape[1]
    total = part_refs[0][...]
    for ref in part_refs[1:]:
        total = total + ref[...]
    high = total.astype(jnp.bfloat16)
    low = (total - high.astype(jnp.float32)).astype(jnp.bfloat16)
    height, lanes = total.shape
    for block_ref in block_refs:
        block_ref[:height, width:] = jnp.concatenate(
            [high[:, : lanes // 2], low[:, : lanes // 2]], axis=1
        )
    for lower, (first_ref, second_ref) in enumerate(
        ((arrived_ref, kept_ref), (kept_ref, arrived_ref))
    ):

        @pl.when(lax.axis_index("sub") == 1 - lower)
        def _():
            for index, step in enumerate(order):
                block_ref = block_refs[step]
                rows = slice(index * cols, (index + 1) * cols)
                block_ref[:cols, :width] = first_ref[rows, :]
                block_ref[cols:, :width] = second_ref[rows, :]


def place_kernel(seq_count, wide, *refs):
    block_refs, (hidden_ref, actions_ref) = refs[:seq_count], refs[seq_count:]
    width = hidden_ref.shape[1]
    lanes = block_refs[0].shape[1] - width
    height = ROLLS * LINES
    total = None
    for step, ref in enumerate(block_refs):
        first = pl.multiple_of((lax.axis_index("seq") ^ step) * wide, wide)
        hidden_ref[pl.ds(first, wide), :] = ref[:, :width]
        part = ref[:height, width:].astype(jnp.float32)
        total = part if total is None else total + part
    total = total[:, : lanes // 2] + total[:, lanes // 2 :]
    outs, _, each = actions_ref.shape
    for roll in range(ROLLS):
        actions_ref[:, roll, :] = total[roll * LINES : roll * LINES + outs, :each]


def fast_shards(frames_in, attn_gain, w_qkv, w_out, vit_gain, w_pair, w_act, pair_frames):
    rows_own, width = frames_in.shape
    seq_count = lax.axis_size("seq")
    head_count = lax.axis_size("head")
    split_count = head_count * 2
    heads, triple = w_qkv.shape[1:]
    head_dim = triple // 3
    wide = rows_own // seq_count
    cols = wide // 2
    patches = rows_own // ROLLS
    vmem = pl.BlockSpec(memory_space=pltpu.VMEM)
    hbm = pl.BlockSpec(memory_space=pltpu.HBM)
    wq_own = jnp.transpose(w_qkv, (1, 2, 0)).reshape(heads * triple, width)
    wa_own = w_act.T
    small = [attn_gain.reshape(-1, 128), vit_gain.reshape(-1, 128), wa_own, pair_frames]
    cut = pl.pallas_call(
        functools.partial(cut_kernel, seq_count, len(small)),
        compiler_params=GRANT,
        in_specs=[hbm] * (1 + len(small)),
        out_specs=[vmem] * (seq_count + len(small)),
        out_shape=[pltpu.VMEM((wide, width), jnp.bfloat16)] * seq_count
        + [pltpu.VMEM(value.shape, value.dtype) for value in small],
        scratch_shapes=[pltpu.SemaphoreType.DMA((seq_count + len(small),))],
    )(off_chip(frames_in), *[off_chip(value) for value in small])
    pieces = cut[:seq_count]
    attn_gain, vit_gain, wa_own, pair_frames = cut[seq_count:]
    cut_pieces = pieces
    pieces = [cut_pieces[0]]
    for step in range(1, seq_count):
        pieces.append(swap(cut_pieces[step], "seq", step))
    wq_pal = swap(wq_own, "sub", 1)
    wo_pal = swap(w_out, "sub", 1)
    wp_pal = swap(w_pair, "sub", 1)
    wa_pal = swap(wa_own, "sub", 1)
    half = pltpu.VMEM((seq_count * cols, width), jnp.bfloat16)
    middle = seq_count // 2
    early = (0, middle) if seq_count > 2 else (0,)
    late = tuple(step for step in range(1, seq_count) if step not in early)
    order = early + late
    batches = []
    for steps in (early, late):
        mine, pals = pl.pallas_call(
            functools.partial(halve_kernel, cols),
            compiler_params=GRANT,
            in_specs=[vmem] * len(steps),
            out_specs=[vmem] * 2,
            out_shape=[pltpu.VMEM((len(steps) * cols, width), jnp.bfloat16)] * 2,
        )(*[pieces[step] for step in steps])
        batch = [mine]
        for step in range(1, split_count):
            batch.append(swap(pals if step & 1 else mine, ("head", "sub"), step))
        batches.append(batch)
    tokens = [batch[step] for step in range(split_count) for batch in batches]
    wq_near, wo_near = pl.pallas_call(
        load_kernel,
        compiler_params=GRANT,
        in_specs=[hbm] * 2,
        out_specs=[vmem] * 2,
        out_shape=[pltpu.VMEM(value.shape, value.dtype) for value in (wq_own, w_out)],
        scratch_shapes=[pltpu.SemaphoreType.DMA((2,))],
    )(off_chip(wq_own), off_chip(w_out))
    rows = split_count * seq_count * cols
    inner = heads * head_dim
    branch = pl.pallas_call(
        functools.partial(attend_kernel, cols, heads, head_dim),
        compiler_params=GRANT,
        in_specs=[vmem] * (2 * split_count + 5),
        out_specs=vmem,
        out_shape=pltpu.VMEM((rows, width), jnp.bfloat16),
        scratch_shapes=[
            pltpu.VMEM((rows, width), jnp.bfloat16),
            pltpu.VMEM((6 * inner, rows), jnp.bfloat16),
            pltpu.VMEM((2 * inner, rows), jnp.bfloat16),
        ],
    )(*tokens, attn_gain, wq_near, wq_pal, wo_near, wo_pal)
    others = [swap(branch, "head", step) for step in range(1, head_count)]
    embed = w_pair.shape[2]
    wanted = pair_frames.shape[1]
    kept, passed, part = pl.pallas_call(
        functools.partial(
            pair_kernel, cols, F, order, split_count, patches, head_count - 1
        ),
        compiler_params=GRANT,
        in_specs=[vmem] * (2 * split_count + head_count + 6),
        out_specs=[vmem] * 3,
        out_shape=(half, half, pltpu.VMEM((ROLLS * LINES, 128), jnp.float32)),
        scratch_shapes=[
            pltpu.VMEM((rows, width), jnp.bfloat16),
            pltpu.VMEM((rows, embed), jnp.float32),
            pltpu.VMEM((rows, embed), jnp.float32),
        ],
    )(
        *tokens, branch, *others, vit_gain, on_chip(w_pair), wp_pal,
        wa_own, wa_pal, pair_frames,
    )
    arrived = swap(passed, "sub", 1)
    parts = [part]
    for step in range(1, split_count):
        parts.append(swap(part, ("head", "sub"), step))
    blocks = pl.pallas_call(
        functools.partial(pack_kernel, cols, order, split_count),
        compiler_params=GRANT,
        in_specs=[vmem] * (2 + split_count),
        out_specs=[vmem] * seq_count,
        out_shape=[pltpu.VMEM((wide, width + 128), jnp.bfloat16)] * seq_count,
    )(kept, arrived, *parts)
    cut_blocks = blocks
    blocks = [cut_blocks[0]]
    for step in range(1, seq_count):
        blocks.append(swap(cut_blocks[step], "seq", step))
    hidden, actions = pl.pallas_call(
        functools.partial(place_kernel, seq_count, wide),
        compiler_params=GRANT,
        in_specs=[vmem] * seq_count,
        out_shape=(
            jax.ShapeDtypeStruct((rows_own, width), jnp.bfloat16),
            jax.ShapeDtypeStruct((w_act.shape[1], ROLLS, wanted), jnp.float32),
        ),
    )(*blocks)
    return hidden, jnp.transpose(actions, (1, 2, 0))


def shards(frames_in, attn_gain, w_qkv, w_out, vit_gain, w_pair, w_act, pair_frames):
    seq_count = lax.axis_size("seq")
    head_count = lax.axis_size("head")
    rows_own = frames_in.shape[0]
    powers = all(count & (count - 1) == 0 for count in (seq_count, head_count))
    one_frame = seq_count * head_count * lax.axis_size("sub") == F
    tiled = rows_own % (seq_count * 16) == 0 and lax.axis_size("sub") == 2
    tiled = tiled and rows_own // seq_count >= ROLLS * LINES
    tiled = tiled and pair_frames.shape[1] <= 64 and w_act.shape[1] <= LINES
    tiled = tiled and frames_in.shape[1] % 128 == 0
    chosen = fast_shards if powers and one_frame and tiled else general_shards
    return chosen(frames_in, attn_gain, w_qkv, w_out, vit_gain, w_pair, w_act, pair_frames)


def solution(mesh):
    in_specs = (
        P(("groups", "seq", "head", "sub"), None),
        P(),
        P(None, ("head", "sub"), None),
        P(("head", "sub"), None),
        P(),
        P(None, None, ("head", "sub")),
        P(("head", "sub"), None),
        P("groups", None),
    )
    out_specs = (P(("groups", "seq", "head", "sub"), None), P("groups", None, None))
    return jax.shard_map(shards, mesh=mesh, in_specs=in_specs, out_specs=out_specs, check_vma=False)
```

```python
import functools

import jax
import jax.numpy as jnp
from jax import lax
from jax.experimental import pallas as pl
from jax.experimental.pallas import tpu as pltpu
from jax.sharding import PartitionSpec as P


F = 16
ROLLS = 2
EPS = 1e-06
LINES = 8


def from_behind(value, axis, steps):
    count = lax.axis_size(axis)
    leading, last = (max(0, -steps), min(count, count - steps))
    return lax.ppermute(value, axis, [(source, source + steps) for source in range(leading, last)])


def normalize(values_in, gain_vec):
    floats = values_in.astype(jnp.float32)
    mean_sq = jnp.mean(floats * floats, axis=-1, keepdims=True)
    return (floats * lax.rsqrt(mean_sq + 1e-06) * gain_vec).astype(jnp.bfloat16)


def general_shards(frames_in, attn_gain, w_qkv, w_out, vit_gain, w_pair, w_act, pair_frames):
    rows_own = frames_in.shape[0]
    model_width = frames_in.shape[1]
    seq_count = lax.axis_size("seq")
    split_count = lax.axis_size(("head", "sub"))
    block_rows = rows_own * split_count
    total_cols = block_rows * seq_count // F
    frames_local = max(1, F // seq_count)
    cols_local = block_rows // frames_local
    frame_step = max(1, seq_count // F)
    heads_local = w_qkv.shape[1]
    triple_dim = w_qkv.shape[2]
    head_dim = triple_dim // 3
    qkv_matrix = w_qkv.reshape(model_width, heads_local * triple_dim)
    normed = lax.all_gather(normalize(frames_in, attn_gain), ("head", "sub"), axis=0, tiled=True)
    qkv_rows = jnp.dot(normed, qkv_matrix, preferred_element_type=jnp.float32).astype(jnp.bfloat16)
    qkv_rows = qkv_rows.reshape(
        frames_local, seq_count, cols_local // seq_count, heads_local, triple_dim
    )
    columns = lax.all_to_all(qkv_rows, "seq", split_axis=1, concat_axis=0, tiled=True)
    item_count = columns.shape[2]
    by_frame = columns.reshape(F, -1, heads_local, triple_dim)
    queries = by_frame[..., :head_dim]
    key_part = by_frame[..., head_dim : 2 * head_dim]
    value_part = by_frame[..., 2 * head_dim :]
    scores = jnp.einsum(
        "fchd,gchd->chfg", queries, key_part, preferred_element_type=jnp.float32
    ) * head_dim ** (-0.5)
    row_peak = jnp.max(scores, axis=-1, keepdims=True)
    weights = jnp.exp(scores - row_peak)
    weights = (weights / jnp.sum(weights, axis=-1, keepdims=True)).astype(jnp.bfloat16)
    mixed_out = jnp.einsum(
        "chfg,gchd->fchd", weights, value_part, preferred_element_type=jnp.float32
    ).astype(jnp.bfloat16)
    mixed_out = mixed_out.reshape(seq_count * frames_local, 1, item_count, heads_local * head_dim)
    attended = lax.all_to_all(mixed_out, "seq", split_axis=0, concat_axis=1, tiled=True)
    attended = attended.reshape(block_rows, heads_local * head_dim)
    branch_sum = lax.psum_scatter(
        jnp.dot(attended, w_out, preferred_element_type=jnp.float32).astype(jnp.bfloat16),
        ("head", "sub"),
        scatter_dimension=0,
        tiled=True,
    ).astype(jnp.float32)
    hidden = (frames_in.astype(jnp.float32) + branch_sum).astype(jnp.bfloat16)
    vit_own = normalize(hidden, vit_gain)
    vit_rows = lax.all_gather(vit_own, ("head", "sub"), axis=0, tiled=True)
    current = jnp.dot(vit_rows, w_pair[0], preferred_element_type=jnp.float32)
    ahead_proj = jnp.dot(vit_rows, w_pair[1], preferred_element_type=jnp.float32)
    ahead_proj = ahead_proj.reshape(frames_local, cols_local, -1)
    arrived = from_behind(ahead_proj[:1].astype(jnp.bfloat16), "seq", -frame_step).astype(
        jnp.float32
    )
    following = jnp.concatenate([ahead_proj[1:], arrived], axis=0).reshape(block_rows, -1)
    embedded = current + following
    activated = jax.nn.gelu(embedded, approximate=False).reshape(frames_local, cols_local, -1)
    seq_index = lax.axis_index("seq")
    first_token = seq_index * block_rows
    frame_first = first_token // total_cols
    col_first = first_token % total_cols
    patches = total_cols // ROLLS
    roll_ids = (col_first + jnp.arange(cols_local, dtype=jnp.int32)) // patches
    member = (roll_ids[None, :] == jnp.arange(ROLLS, dtype=jnp.int32)[:, None]).astype(
        jnp.float32
    ) / patches
    pooled = jnp.einsum("rp,fpe->fre", member, activated, precision=lax.Precision.HIGHEST)
    scored = jnp.einsum("fre,ea->fra", pooled, w_act, precision=lax.Precision.HIGHEST)
    frame_ids = frame_first + jnp.arange(frames_local, dtype=jnp.int32)
    selector = (pair_frames[:, :, None] == frame_ids[None, None, :]).astype(jnp.float32)
    partial_value = jnp.einsum("rjf,fra->rja", selector, scored, precision=lax.Precision.HIGHEST)
    actions = lax.psum(partial_value, ("seq", "head", "sub"))
    return (hidden, actions)


GRANT = pltpu.CompilerParams(vmem_limit_bytes=12 * 1024 * 1024)


def on_chip(value):
    return pltpu.with_memory_space_constraint(value, pltpu.VMEM)


def off_chip(value):
    return pltpu.with_memory_space_constraint(value, pltpu.HBM)


def swap(value, axis, mask):
    count = lax.axis_size(axis)
    pairs = [(source, source ^ mask) for source in range(count)]
    return on_chip(lax.ppermute(value, axis, pairs))


def lined(gain_ref):
    return jnp.concatenate([gain_ref[row : row + 1, :] for row in range(gain_ref.shape[0])], axis=1)


def scaled(rows, gain_row):
    mean_sq = jnp.mean(rows * rows, axis=-1, keepdims=True)
    return (rows * lax.rsqrt(mean_sq + EPS) * gain_row).astype(jnp.bfloat16)


def cut_kernel(tokens_ref, *refs):
    out_refs, sems = refs[:-1], refs[-1]
    wide = out_refs[0].shape[0]
    place = lax.axis_index("seq")
    copies = []
    for step, out_ref in enumerate(out_refs):
        first = pl.multiple_of((place ^ step) * wide, wide)
        source = tokens_ref.at[pl.ds(first, wide), :]
        copies.append(pltpu.make_async_copy(source, out_ref, sems.at[step]))
    for copy in copies:
        copy.start()
    for copy in copies:
        copy.wait()


def halve_kernel(cols, *refs):
    *piece_refs, mine_ref, pals_ref = refs
    for lower, (first_ref, second_ref) in enumerate(((pals_ref, mine_ref), (mine_ref, pals_ref))):

        @pl.when(lax.axis_index("sub") == 1 - lower)
        def _():
            for step, ref in enumerate(piece_refs):
                rows = slice(step * cols, (step + 1) * cols)
                first_ref[rows, :] = ref[:cols, :]
                second_ref[rows, :] = ref[cols:, :]


def aligned(value, step):
    return value if isinstance(value, int) else pl.multiple_of(value, step)


def each(count, body):
    lax.fori_loop(0, count, lambda index, carry: (body(index), carry)[1], 0)


def load_kernel(*refs):
    *refs, sems = refs
    half = len(refs) // 2
    copies = [
        pltpu.make_async_copy(refs[index], refs[half + index], sems.at[index])
        for index in range(half)
    ]
    for copy in copies:
        copy.start()
    for copy in copies:
        copy.wait()


def attend_kernel(cols, heads, head_dim, *refs):
    *token_refs, gain_ref, wq_own, wq_pal, wo_own, wo_pal, out_ref = refs[:-3]
    normed_ref, qkv_ref, mixed_ref = refs[-3:]
    triple = 3 * head_dim
    inner = heads * head_dim
    group = 2 if heads % 2 == 0 else 1
    gain_row = lined(gain_ref)
    first = 0
    for ref in token_refs:
        normed_ref[first : first + ref.shape[0], :] = scaled(
            ref[...].astype(jnp.float32), gain_row
        )
        first += ref.shape[0]
    rows = normed_ref.shape[0]

    def project(wq_ref, source, size, target):
        qkv_ref[pl.ds(aligned(target, head_dim), size), :] = lax.dot_general(
            wq_ref[pl.ds(aligned(source, size), size), :], normed_ref[...],
            (((1,), (1,)), ((), ())), preferred_element_type=jnp.float32,
        ).astype(jnp.bfloat16)

    large = heads * triple // group

    def project_both(index):
        project(wq_pal, index * large, large, index * large)
        project(wq_own, index * large, large, heads * triple + index * large)

    each(group, project_both)
    left = lax.broadcasted_iota(jnp.int32, (rows, rows), 0) % cols
    right = lax.broadcasted_iota(jnp.int32, (rows, rows), 1) % cols
    same = left == right
    for head in range(2 * heads):
        base = head * triple
        query = qkv_ref[base : base + head_dim, :]
        key = qkv_ref[base + head_dim : base + 2 * head_dim, :]
        val = qkv_ref[base + 2 * head_dim : base + triple, :]
        scores = lax.dot_general(
            key, query, (((0,), (0,)), ((), ())), preferred_element_type=jnp.float32
        ) * head_dim ** (-0.5)
        scores = jnp.where(same, scores, -jnp.inf)
        weights = jnp.exp(scores - jnp.max(scores, axis=0, keepdims=True))
        weights = weights * (1.0 / jnp.sum(weights, axis=0, keepdims=True))
        mixed_ref[head * head_dim : (head + 1) * head_dim, :] = jnp.dot(
            val, weights.astype(jnp.bfloat16), preferred_element_type=jnp.float32
        ).astype(jnp.bfloat16)
    total = None
    for index, wo_ref in enumerate((wo_pal, wo_own)):
        product = lax.dot_general(
            mixed_ref[index * inner : (index + 1) * inner, :], wo_ref[...],
            (((0,), (0,)), ((), ())), preferred_element_type=jnp.float32,
        ).astype(jnp.bfloat16).astype(jnp.float32)
        total = product if total is None else total + product
    out_ref[...] = total.astype(jnp.bfloat16)


def pair_kernel(cols, frames, order, split_count, patches, others, *refs):
    batches = 2 * split_count
    token_refs, refs = refs[:batches], refs[batches:]
    own_ref, refs = refs[0], refs[1:]
    other_refs, refs = refs[:others], refs[others:]
    gain_ref, wp_a, wp_b, wa_a, wa_b, pairs_ref, keep_ref, pass_ref, part_ref, *refs = refs
    hidden_ref, cur_ref, fol_ref = refs
    seq_count = len(order)
    step = seq_count * cols
    seq_place = lax.axis_index("seq")
    split_place = lax.axis_index(("head", "sub"))
    roll = (seq_place * 2 + lax.axis_index("sub")) * cols // patches
    for place in range(split_count):
        first = place * step
        for ref in token_refs[2 * place : 2 * place + 2]:
            height = ref.shape[0]
            rows = slice(first, first + height)
            branch = own_ref[rows, :].astype(jnp.float32)
            for index, other in enumerate(other_refs):
                there = first + ((place ^ (2 * (index + 1))) - place) * step
                branch = branch + other[there : there + height, :].astype(jnp.float32)
            hidden_ref[rows, :] = (ref[...].astype(jnp.float32) + branch).astype(jnp.bfloat16)
            first += height
    keep_ref[...] = hidden_ref[:step, :]
    pass_ref[...] = hidden_ref[step : 2 * step, :]
    vit = scaled(hidden_ref[...].astype(jnp.float32), lined(gain_ref))
    scored = None
    for wp_ref, wa_ref in ((wp_a, wa_a), (wp_b, wa_b)):
        current = jnp.dot(vit, wp_ref[0], preferred_element_type=jnp.float32)
        ahead = jnp.dot(vit, wp_ref[1], preferred_element_type=jnp.float32)
        for split in range(split_count):
            for index, seq in enumerate(order):
                frame = (seq_place ^ seq) * split_count + (split_place ^ split)
                first = (split * seq_count + index) * cols
                piece = slice(first, first + cols)
                place = pl.ds(pl.multiple_of(frame * cols, cols), cols)
                cur_ref[place, :] = current[piece, :]
                fol_ref[place, :] = ahead[piece, :]
        embedded = cur_ref[: (frames - 1) * cols, :] + fol_ref[cols:, :]
        activated = 0.5 * embedded * (1.0 + lax.erf(embedded * (0.5**0.5)))
        pooled = jnp.sum(activated.reshape(frames - 1, cols, -1), axis=1) * (1.0 / patches)
        here = lax.dot_general(
            wa_ref[...], pooled, (((1,), (1,)), ((), ())),
            preferred_element_type=jnp.float32, precision=lax.Precision.HIGHEST,
        )
        scored = here if scored is None else scored + here
    wanted = pairs_ref.shape[1]
    part_ref[...] = jnp.zeros_like(part_ref)
    for index in range(ROLLS):
        chosen = pairs_ref[index : index + 1, :] == lax.broadcasted_iota(
            jnp.int32, (frames - 1, wanted), 0
        )
        first = index * LINES
        part_ref[first : first + scored.shape[0], :wanted] = jnp.dot(
            scored, jnp.where(chosen & (roll == index), 1.0, 0.0),
            preferred_element_type=jnp.float32, precision=lax.Precision.HIGHEST,
        )


def pack_kernel(cols, order, parts, kept_ref, arrived_ref, *refs):
    part_refs, block_refs = refs[:parts], refs[parts:]
    width = kept_ref.shape[1]
    total = part_refs[0][...]
    for ref in part_refs[1:]:
        total = total + ref[...]
    high = total.astype(jnp.bfloat16)
    low = (total - high.astype(jnp.float32)).astype(jnp.bfloat16)
    height, lanes = total.shape
    for block_ref in block_refs:
        block_ref[:height, width:] = jnp.concatenate(
            [high[:, : lanes // 2], low[:, : lanes // 2]], axis=1
        )
    for lower, (first_ref, second_ref) in enumerate(
        ((arrived_ref, kept_ref), (kept_ref, arrived_ref))
    ):

        @pl.when(lax.axis_index("sub") == 1 - lower)
        def _():
            for index, step in enumerate(order):
                block_ref = block_refs[step]
                rows = slice(index * cols, (index + 1) * cols)
                block_ref[:cols, :width] = first_ref[rows, :]
                block_ref[cols:, :width] = second_ref[rows, :]


def place_kernel(seq_count, wide, *refs):
    block_refs, (hidden_ref, actions_ref) = refs[:seq_count], refs[seq_count:]
    width = hidden_ref.shape[1]
    lanes = block_refs[0].shape[1] - width
    height = ROLLS * LINES
    total = None
    for step, ref in enumerate(block_refs):
        first = pl.multiple_of((lax.axis_index("seq") ^ step) * wide, wide)
        hidden_ref[pl.ds(first, wide), :] = ref[:, :width]
        part = ref[:height, width:].astype(jnp.float32)
        total = part if total is None else total + part
    total = total[:, : lanes // 2] + total[:, lanes // 2 :]
    outs, _, each = actions_ref.shape
    for roll in range(ROLLS):
        actions_ref[:, roll, :] = total[roll * LINES : roll * LINES + outs, :each]


def fast_shards(frames_in, attn_gain, w_qkv, w_out, vit_gain, w_pair, w_act, pair_frames):
    rows_own, width = frames_in.shape
    seq_count = lax.axis_size("seq")
    head_count = lax.axis_size("head")
    split_count = head_count * 2
    heads, triple = w_qkv.shape[1:]
    head_dim = triple // 3
    wide = rows_own // seq_count
    cols = wide // 2
    patches = rows_own // ROLLS
    vmem = pl.BlockSpec(memory_space=pltpu.VMEM)
    hbm = pl.BlockSpec(memory_space=pltpu.HBM)
    wq_own = jnp.transpose(w_qkv, (1, 2, 0)).reshape(heads * triple, width)
    wa_own = w_act.T
    pieces = pl.pallas_call(
        cut_kernel,
        compiler_params=GRANT,
        in_specs=[hbm],
        out_specs=[vmem] * seq_count,
        out_shape=[pltpu.VMEM((wide, width), jnp.bfloat16)] * seq_count,
        scratch_shapes=[pltpu.SemaphoreType.DMA((seq_count,))],
    )(off_chip(frames_in))
    cut_pieces = pieces
    pieces = [cut_pieces[0]]
    for step in range(1, seq_count):
        pieces.append(swap(cut_pieces[step], "seq", step))
    wq_pal = swap(wq_own, "sub", 1)
    wo_pal = swap(w_out, "sub", 1)
    wp_pal = swap(w_pair, "sub", 1)
    wa_pal = swap(wa_own, "sub", 1)
    half = pltpu.VMEM((seq_count * cols, width), jnp.bfloat16)
    middle = seq_count // 2
    early = (0, middle) if seq_count > 2 else (0,)
    late = tuple(step for step in range(1, seq_count) if step not in early)
    order = early + late
    batches = []
    for steps in (early, late):
        mine, pals = pl.pallas_call(
            functools.partial(halve_kernel, cols),
            compiler_params=GRANT,
            in_specs=[vmem] * len(steps),
            out_specs=[vmem] * 2,
            out_shape=[pltpu.VMEM((len(steps) * cols, width), jnp.bfloat16)] * 2,
        )(*[pieces[step] for step in steps])
        batch = [mine]
        for step in range(1, split_count):
            batch.append(swap(pals if step & 1 else mine, ("head", "sub"), step))
        batches.append(batch)
    tokens = [batch[step] for step in range(split_count) for batch in batches]
    loads = [
        wq_own, w_out, attn_gain.reshape(-1, 128), vit_gain.reshape(-1, 128), wa_own, pair_frames
    ]
    wq_near, wo_near, attn_gain, vit_gain, wa_near, pair_frames = pl.pallas_call(
        load_kernel,
        compiler_params=GRANT,
        in_specs=[hbm] * len(loads),
        out_specs=[vmem] * len(loads),
        out_shape=[pltpu.VMEM(value.shape, value.dtype) for value in loads],
        scratch_shapes=[pltpu.SemaphoreType.DMA((len(loads),))],
    )(*[off_chip(value) for value in loads])
    rows = split_count * seq_count * cols
    inner = heads * head_dim
    branch = pl.pallas_call(
        functools.partial(attend_kernel, cols, heads, head_dim),
        compiler_params=GRANT,
        in_specs=[vmem] * (2 * split_count + 5),
        out_specs=vmem,
        out_shape=pltpu.VMEM((rows, width), jnp.bfloat16),
        scratch_shapes=[
            pltpu.VMEM((rows, width), jnp.bfloat16),
            pltpu.VMEM((6 * inner, rows), jnp.bfloat16),
            pltpu.VMEM((2 * inner, rows), jnp.bfloat16),
        ],
    )(*tokens, attn_gain, wq_near, wq_pal, wo_near, wo_pal)
    others = [swap(branch, "head", step) for step in range(1, head_count)]
    embed = w_pair.shape[2]
    wanted = pair_frames.shape[1]
    kept, passed, part = pl.pallas_call(
        functools.partial(
            pair_kernel, cols, F, order, split_count, patches, head_count - 1
        ),
        compiler_params=GRANT,
        in_specs=[vmem] * (2 * split_count + head_count + 6),
        out_specs=[vmem] * 3,
        out_shape=(half, half, pltpu.VMEM((ROLLS * LINES, 128), jnp.float32)),
        scratch_shapes=[
            pltpu.VMEM((rows, width), jnp.bfloat16),
            pltpu.VMEM((rows, embed), jnp.float32),
            pltpu.VMEM((rows, embed), jnp.float32),
        ],
    )(
        *tokens, branch, *others, vit_gain, on_chip(w_pair), wp_pal,
        wa_near, wa_pal, pair_frames,
    )
    arrived = swap(passed, "sub", 1)
    parts = [part]
    for step in range(1, split_count):
        parts.append(swap(part, ("head", "sub"), step))
    blocks = pl.pallas_call(
        functools.partial(pack_kernel, cols, order, split_count),
        compiler_params=GRANT,
        in_specs=[vmem] * (2 + split_count),
        out_specs=[vmem] * seq_count,
        out_shape=[pltpu.VMEM((wide, width + 128), jnp.bfloat16)] * seq_count,
    )(kept, arrived, *parts)
    cut_blocks = blocks
    blocks = [cut_blocks[0]]
    for step in range(1, seq_count):
        blocks.append(swap(cut_blocks[step], "seq", step))
    hidden, actions = pl.pallas_call(
        functools.partial(place_kernel, seq_count, wide),
        compiler_params=GRANT,
        in_specs=[vmem] * seq_count,
        out_shape=(
            jax.ShapeDtypeStruct((rows_own, width), jnp.bfloat16),
            jax.ShapeDtypeStruct((w_act.shape[1], ROLLS, wanted), jnp.float32),
        ),
    )(*blocks)
    return hidden, jnp.transpose(actions, (1, 2, 0))


def shards(frames_in, attn_gain, w_qkv, w_out, vit_gain, w_pair, w_act, pair_frames):
    seq_count = lax.axis_size("seq")
    head_count = lax.axis_size("head")
    rows_own = frames_in.shape[0]
    powers = all(count & (count - 1) == 0 for count in (seq_count, head_count))
    one_frame = seq_count * head_count * lax.axis_size("sub") == F
    tiled = rows_own % (seq_count * 16) == 0 and lax.axis_size("sub") == 2
    tiled = tiled and rows_own // seq_count >= ROLLS * LINES
    tiled = tiled and pair_frames.shape[1] <= 64 and w_act.shape[1] <= LINES
    tiled = tiled and frames_in.shape[1] % 128 == 0
    chosen = fast_shards if powers and one_frame and tiled else general_shards
    return chosen(frames_in, attn_gain, w_qkv, w_out, vit_gain, w_pair, w_act, pair_frames)


def solution(mesh):
    in_specs = (
        P(("groups", "seq", "head", "sub"), None),
        P(),
        P(None, ("head", "sub"), None),
        P(("head", "sub"), None),
        P(),
        P(None, None, ("head", "sub")),
        P(("head", "sub"), None),
        P("groups", None),
    )
    out_specs = (P(("groups", "seq", "head", "sub"), None), P("groups", None, None))
    return jax.shard_map(shards, mesh=mesh, in_specs=in_specs, out_specs=out_specs, check_vma=False)
```
